32 devices in a mesh: pipe: 2 (over core), expert: 16 (over z, y, x).
Axes of the slice: x: 2, y: 2, z: 4, core: 2. Of those that a mesh axis runs over, the one named last changes fastest.
Arguments:
- tokens: bfloat16 [4096, 2048], P(('pipe', 'expert')), may hold values from -6 to 6
- routes: int32 [4096, 8], P(('pipe', 'expert')), may hold values from 0 to 15, all different within a row; in each aligned block of 128 rows (0 to 127, 128 to 255, ...) at most 64 rows name the same one
- gates: float32 [4096, 8], P(('pipe', 'expert')), may hold values from 0.1 to 1
- cotangent: bfloat16 [4096, 2048], P(('pipe', 'expert')), may hold values from -1.5 to 1.5
- w_gate: bfloat16 [16, 2048, 384], P('expert'), may hold values from -0.125 to 0.125
- w_up: bfloat16 [16, 2048, 384], P('expert'), may hold values from -0.125 to 0.125
- w_down: bfloat16 [16, 384, 2048], P('expert'), may hold values from -0.3125 to 0.3125
Outputs:
- mixed: bfloat16 [4096, 2048], P(('pipe', 'expert'))
- input_grad: bfloat16 [4096, 2048], P(('pipe', 'expert'))
- gate_weight_grad: bfloat16 [16, 2048, 384], P('expert')
- up_weight_grad: bfloat16 [16, 2048, 384], P('expert')
- down_weight_grad: bfloat16 [16, 384, 2048], P('expert')
The draws below stay inside these ranges and needn't reach their ends.
Inputs may be any that keep to these rules, and one draw needn't show every extreme that they name: `routes`: each row names 8 different experts. Within the rows of one device (aligned blocks of 128 rows, device order pipe then expert) each expert is named exactly 64 times.
All inputs are finite; a program needn't handle non-finite values.
Results may differ from the reference program's by a relative error of at most 0.009.
Values may be sent and summed in bfloat16 or wider, within the bound.
No kernel may reach another device: no remote copies, remote signals or barrier semaphores. Data moves between devices by JAX's collectives and lax.ppermute only.
A program may use at most 128 MiB of HBM per device.

```python
import math
import jax
import jax.numpy as jnp
import numpy as np
from jax import lax

D = 2048
FF = 384
TOP = 8
TOK_DEV = 128
EXPERTS = 16
CAP = 64
TOKENS = 4096
N_PIPE = 2
N_EXPERT = 16


def block_levels(rng, extent, shards, least, largest):
    def one(dim, blocks):
        draws = jax.random.uniform(jax.random.fold_in(jax.random.fold_in(rng, 6), dim), (blocks,), jnp.float32, least / len(shards), largest / len(shards))
        return jnp.repeat(jnp.exp(draws), extent[dim] // blocks).reshape((-1,) + (1,) * (len(extent) - dim - 1))

    gain = one(*shards[0])
    for cut in shards[1:]:
        gain = gain * one(*cut)
    return gain


def shared_out(rng, own, number, rows, amount, top, bound, slope):
    sequence = jax.random.permutation(rng, amount)
    packed, usual = portions_of(amount, rows * top, bound, slope, True), portions_of(amount, rows * top, bound, slope, False)
    places = jnp.arange(amount)

    def named(sizes, turn):
        used = int((sizes > 0).sum())
        fixed = max(1, used // 4)
        shifted = fixed + (places - fixed + turn * (used - fixed)) % max(1, amount - fixed)
        return jnp.zeros((amount,), jnp.int32).at[sequence[jnp.where(places < fixed, places, shifted)]].set(jnp.asarray(sizes, jnp.int32))

    sizes = jnp.where(number % 4 == 0, named(packed, number // 4), named(usual, number - number // 4 - 1))
    mixed = jax.random.permutation(jax.random.fold_in(own, 3), amount)
    giver, taker = mixed[0:amount // 2 * 2:2], mixed[1:amount // 2 * 2:2]
    room = jnp.minimum(sizes[giver] - 1, bound - sizes[taker]) // 2
    room = jnp.where((giver == sequence[0]) | (taker == sequence[0]) | (sizes[taker] == 0), 0, jnp.maximum(room, 0))
    shifted = jax.random.randint(jax.random.fold_in(own, 4), (amount // 2,), 0, 1 << 20) % (room + 1)
    sizes = sizes.at[giver].add(-shifted).at[taker].add(shifted)
    members = jnp.searchsorted(jnp.cumsum(sizes), jnp.arange(rows * top), side="right").astype(jnp.int32)
    grid = members.reshape(top, rows).T
    grid = grid[jax.random.permutation(jax.random.fold_in(own, 1), rows)]
    turn = jax.random.randint(jax.random.fold_in(own, 2), (rows, 1), 0, top)
    return jnp.take_along_axis(grid, (jnp.arange(top)[None, :] + turn) % top, axis=1)


def portions_of(number_of, total, bound, slope, full):
    weights = [(1 << 20) // math.isqrt(standing ** slope) + 1 for standing in range(1, number_of + 1)]
    largest = bound if full else min(bound, max(-(-total // number_of), total * weights[0] // sum(weights)))
    least = 1 if total - largest >= number_of - 1 else 0
    counts, rest = [largest] + [least] * (number_of - 1), total - largest - least * (number_of - 1)
    while rest > 0:
        candidates = [i for i in range(1, number_of) if counts[i] < largest] or [i for i in range(1, number_of) if counts[i] < bound]
        mass, remaining = sum([weights[i] for i in candidates]), rest
        for i in candidates:
            more = min(bound - counts[i], max(1, remaining * weights[i] // mass), rest)
            counts[i] = counts[i] + more
            rest = rest - more
    return np.array(counts)


def centred(stream_key, shape, scale, reach, cuts=(), held_as=jnp.bfloat16):
    entries = jax.random.normal(stream_key, shape, jnp.float32) * scale
    if len(cuts) > 0:
        entries = block_levels(stream_key, shape, cuts, -0.22, 0.18) * entries
    return jnp.clip(entries, min=-reach, max=reach).astype(held_as)


def setup_inputs(seed: int = 0) -> dict:
    seeds = jax.random.split(jax.random.key(seed), 8)
    tokens = centred(seeds[0], (TOKENS, D), 1.0, 6.0, ((0, 32),))
    routes_keys = jax.random.split(jax.random.fold_in(seeds[1], 1), TOKENS // TOK_DEV)
    routes_turns = jax.random.permutation(jax.random.fold_in(seeds[1], 3), TOKENS // TOK_DEV)
    routes = jax.vmap(lambda own, number: shared_out(jax.random.fold_in(seeds[1], 2), own, number, TOK_DEV, EXPERTS, TOP, CAP, 2))(routes_keys, routes_turns).reshape((TOKENS, TOP))
    gates = jnp.clip(0.1 + 0.9 * jax.random.uniform(seeds[2], (TOKENS, TOP), jnp.float32) ** block_levels(seeds[2], (TOKENS, TOP), ((0, 32),), -0.2, 0.2), 0.1, 1.0)
    cotangent = centred(seeds[3], (TOKENS, D), 0.25, 1.5, ((0, 32),))
    w_gate = centred(seeds[4], (EXPERTS, D, FF), D ** -0.5, 0.125, ((0, 16),))
    w_up = centred(seeds[5], (EXPERTS, D, FF), D ** -0.5, 0.125, ((0, 16),))
    w_down = centred(seeds[6], (EXPERTS, FF, D), FF ** -0.5, 0.3125, ((0, 16),))
    return {"tokens": tokens, "routes": routes, "gates": gates, "cotangent": cotangent, "w_gate": w_gate, "w_up": w_up, "w_down": w_down}


def slot_index(block_routes, expert_count, capacity):
    flat = block_routes.reshape(-1).astype(jnp.int32)
    onehot = (flat[:, None] == jnp.arange(expert_count, dtype=jnp.int32)[None, :]).astype(jnp.int32)
    before = jnp.cumsum(onehot, axis=0) - onehot
    ranks = jnp.sum(before * onehot, axis=1).astype(jnp.int32)
    return (flat * capacity + ranks).astype(jnp.int32)


def pick_rows(table, index):
    return table[index]


def reference(tokens, routes, gates, cotangent, w_gate, w_up, w_down):
    groups = N_PIPE * N_EXPERT
    blocks = routes.reshape(groups, TOK_DEV, TOP)
    slots = jax.vmap(lambda block: slot_index(block, EXPERTS, CAP))(blocks)
    source = (jnp.arange(groups, dtype=jnp.int32) % N_EXPERT)[:, None]
    target = (slots // CAP) * (N_EXPERT * CAP) + source * CAP + slots % CAP
    token_rows = source * TOK_DEV + (jnp.arange(TOK_DEV * TOP, dtype=jnp.int32) // TOP)[None, :]
    target = target.reshape(N_PIPE, -1).astype(jnp.int32)
    token_rows = token_rows.reshape(N_PIPE, -1).astype(jnp.int32)
    gate_flat = gates.reshape(N_PIPE, -1)
    pipe_rows = N_EXPERT * TOK_DEV
    total_slots = EXPERTS * N_EXPERT * CAP
    per_expert = N_EXPERT * CAP
    token_of = jax.vmap(lambda where, what: jnp.full((total_slots,), pipe_rows, jnp.int32).at[where].set(what))(target, token_rows)
    weight_of = jax.vmap(lambda where, what: jnp.zeros((total_slots,), jnp.float32).at[where].set(what))(target, gate_flat)
    token_of = token_of.reshape(N_PIPE, EXPERTS, per_expert).transpose(1, 0, 2)
    weight_of = weight_of.reshape(N_PIPE, EXPERTS, per_expert).transpose(1, 0, 2)
    token_pad = jnp.concatenate([tokens.reshape(N_PIPE, pipe_rows, D), jnp.zeros((N_PIPE, 1, D), tokens.dtype)], axis=1)
    cot_pad = jnp.concatenate([cotangent.reshape(N_PIPE, pipe_rows, D), jnp.zeros((N_PIPE, 1, D), cotangent.dtype)], axis=1)
    pipe_index = jnp.broadcast_to(jnp.arange(N_PIPE, dtype=jnp.int32)[:, None], (N_PIPE, per_expert))

    def one_expert(carry, operands):
        mixed_acc, grad_acc = carry
        index, weights, gate_mat, up_mat, down_mat = operands
        inputs = jax.vmap(pick_rows)(token_pad, index).reshape(-1, D)
        cots = jax.vmap(pick_rows)(cot_pad, index).reshape(-1, D)
        weight_col = weights.reshape(-1)[:, None]
        gate_pre = jnp.dot(inputs, gate_mat, preferred_element_type=jnp.float32)
        up_pre = jnp.dot(inputs, up_mat, preferred_element_type=jnp.float32)
        sigma = jax.nn.sigmoid(gate_pre)
        hidden = (gate_pre * sigma * up_pre).astype(jnp.bfloat16)
        outputs = jnp.dot(hidden, down_mat, preferred_element_type=jnp.float32).astype(jnp.bfloat16)
        slot_cot = (weight_col * cots.astype(jnp.float32)).astype(jnp.bfloat16)
        hidden_grad = jnp.dot(slot_cot, down_mat.T, preferred_element_type=jnp.float32)
        gate_grad = (hidden_grad * up_pre * sigma * (1.0 + gate_pre * (1.0 - sigma))).astype(jnp.bfloat16)
        up_grad = (hidden_grad * gate_pre * sigma).astype(jnp.bfloat16)
        slot_grads = (jnp.dot(gate_grad, gate_mat.T, preferred_element_type=jnp.float32)
                      + jnp.dot(up_grad, up_mat.T, preferred_element_type=jnp.float32)).astype(jnp.bfloat16)
        contrib = (weight_col * outputs.astype(jnp.float32)).reshape(N_PIPE, per_expert, D)
        mixed_acc = mixed_acc.at[pipe_index, index].add(contrib)
        grad_acc = grad_acc.at[pipe_index, index].add(slot_grads.astype(jnp.float32).reshape(N_PIPE, per_expert, D))
        inputs_f = inputs.astype(jnp.float32).reshape(N_PIPE, per_expert, D)
        hidden_f = hidden.astype(jnp.float32).reshape(N_PIPE, per_expert, FF)
        cot_f = slot_cot.astype(jnp.float32).reshape(N_PIPE, per_expert, D)
        gate_f = gate_grad.astype(jnp.float32).reshape(N_PIPE, per_expert, FF)
        up_f = up_grad.astype(jnp.float32).reshape(N_PIPE, per_expert, FF)
        down_part = jnp.einsum('pmf,pmd->pfd', hidden_f, cot_f).astype(jnp.bfloat16).astype(jnp.float32)
        gate_part = jnp.einsum('pmd,pmf->pdf', inputs_f, gate_f).astype(jnp.bfloat16).astype(jnp.float32)
        up_part = jnp.einsum('pmd,pmf->pdf', inputs_f, up_f).astype(jnp.bfloat16).astype(jnp.float32)
        sums = (jnp.sum(gate_part, axis=0).astype(jnp.bfloat16),
                jnp.sum(up_part, axis=0).astype(jnp.bfloat16),
                jnp.sum(down_part, axis=0).astype(jnp.bfloat16))
        return (mixed_acc, grad_acc), sums

    start = (jnp.zeros((N_PIPE, pipe_rows + 1, D), jnp.float32), jnp.zeros((N_PIPE, pipe_rows + 1, D), jnp.float32))
    (mixed_acc, grad_acc), grads = lax.scan(one_expert, start, (token_of, weight_of, w_gate, w_up, w_down))
    mixed = mixed_acc[:, :pipe_rows].reshape(TOKENS, D).astype(jnp.bfloat16)
    input_grad = grad_acc[:, :pipe_rows].reshape(TOKENS, D).astype(jnp.bfloat16)
    return (mixed, input_grad, grads[0], grads[1], grads[2])
```

```python
import functools

import jax
import jax.numpy as jnp
from jax import lax
from jax.experimental import pallas as pl
from jax.experimental.pallas import tpu as pltpu
from jax.sharding import PartitionSpec as P

PLANE = 4
BF = jnp.bfloat16
F32 = jnp.float32


def slot_index(block_routes, expert_count, capacity):
    flat = block_routes.reshape(-1)
    onehot = (flat[:, None] == jnp.arange(expert_count, dtype=jnp.int32)[None, :]).astype(jnp.int32)
    before = jnp.cumsum(onehot, axis=0) - onehot
    ranks = jnp.sum(before * onehot, axis=1)
    return flat * capacity + ranks


def expert_forward(block, gate_mat, up_mat, down_mat):
    inputs = block.reshape(-1, block.shape[2])
    gate_pre = jnp.dot(inputs, gate_mat, preferred_element_type=jnp.float32)
    up_pre = jnp.dot(inputs, up_mat, preferred_element_type=jnp.float32)
    sigma = jax.nn.sigmoid(gate_pre)
    hidden = (gate_pre * sigma * up_pre).astype(jnp.bfloat16)
    outputs = jnp.dot(hidden, down_mat, preferred_element_type=jnp.float32).astype(jnp.bfloat16)
    return (gate_pre, up_pre, hidden, outputs)


def direct_plan(tokens, routes, gates, cotangent, w_gate, w_up, w_down):
    rows_dev, width = tokens.shape
    picks = routes.shape[1]
    experts = lax.axis_size("expert")
    capacity = rows_dev * picks // experts
    gate_mat = w_gate[0]
    up_mat = w_up[0]
    down_mat = w_down[0]
    slots = slot_index(routes, experts, capacity)
    flat_rows = jnp.arange(rows_dev * picks, dtype=jnp.int32) // picks
    token_of = jnp.full((experts * capacity,), rows_dev, jnp.int32).at[slots].set(flat_rows)
    weight_of = jnp.zeros((experts * capacity,), jnp.float32).at[slots].set(gates.reshape(-1))
    token_pad = jnp.concatenate([tokens, jnp.zeros((1, width), tokens.dtype)], axis=0)
    send = token_pad[token_of].reshape(experts, capacity, width)

    def exchange(rows):
        return lax.all_to_all(
            rows.reshape(experts, capacity, width), "expert", split_axis=0, concat_axis=0, tiled=True
        )

    block = exchange(send)
    gate_pre, up_pre, hidden, outputs = expert_forward(block, gate_mat, up_mat, down_mat)
    back_items = exchange(outputs)
    inputs = block.reshape(-1, width)
    gathered = back_items.reshape(-1, width)[slots].reshape(rows_dev, picks, width)
    mixed = jnp.sum(gates[:, :, None] * gathered.astype(jnp.float32), axis=1).astype(jnp.bfloat16)
    cot_pad = jnp.concatenate([cotangent, jnp.zeros((1, width), cotangent.dtype)], axis=0)
    cot_send = (weight_of[:, None] * cot_pad[token_of].astype(jnp.float32)).astype(jnp.bfloat16)
    slot_cot = exchange(cot_send).reshape(-1, width)
    down_part = jnp.dot(hidden.T, slot_cot, preferred_element_type=jnp.float32)
    hidden_grad = jnp.dot(slot_cot, down_mat.T, preferred_element_type=jnp.float32)
    sigma = jax.nn.sigmoid(gate_pre)
    gate_grad = (hidden_grad * up_pre * sigma * (1.0 + gate_pre * (1.0 - sigma))).astype(
        jnp.bfloat16
    )
    up_grad = (hidden_grad * gate_pre * sigma).astype(jnp.bfloat16)
    slot_grads = (
        jnp.dot(gate_grad, gate_mat.T, preferred_element_type=jnp.float32)
        + jnp.dot(up_grad, up_mat.T, preferred_element_type=jnp.float32)
    ).astype(jnp.bfloat16)
    grads_back = exchange(slot_grads)
    gate_part = jnp.dot(inputs.T, gate_grad, preferred_element_type=jnp.float32)
    up_part = jnp.dot(inputs.T, up_grad, preferred_element_type=jnp.float32)
    grad_rows = grads_back.reshape(-1, width)[slots].reshape(rows_dev, picks, width)
    input_grad = jnp.sum(grad_rows.astype(jnp.float32), axis=1).astype(jnp.bfloat16)
    return (mixed, input_grad) + relay_sums(gate_part, up_part, down_part)


def relay_sums(*parts):
    relays = lax.axis_size("pipe")
    sums = []
    for part in parts:
        part = part.astype(BF)
        if relays == 2:
            other = lax.ppermute(part, "pipe", [(0, 1), (1, 0)])
            total = (part.astype(F32) + other.astype(F32)).astype(BF)
        else:
            total = lax.psum(part, "pipe")
        sums.append(total[None])
    return tuple(sums)


def pick_matrix(ids_ref, meta, k, capacity):
    picks, rows = meta.shape[0] // 2, meta.shape[1]
    hit = meta[:picks] == ids_ref[k].astype(F32)
    weight = jnp.sum(jnp.where(hit, meta[picks:], 0.0), axis=0, keepdims=True)
    member = jnp.sum(jnp.where(hit, 1.0, 0.0), axis=0, keepdims=True)
    first = lax.broadcasted_iota(jnp.int32, (rows, rows), 0)
    second = lax.broadcasted_iota(jnp.int32, (rows, rows), 1)
    ahead = jnp.where(first < second, 1.0, 0.0).astype(BF)
    member8 = jnp.broadcast_to(member, (16, rows)).astype(BF)
    rank = jnp.dot(member8, ahead, preferred_element_type=F32)[0:1]
    place = jnp.where(member > 0.5, rank, -1.0)
    slot = lax.broadcasted_iota(jnp.int32, (capacity, rows), 0).astype(F32)
    return slot == place, weight


def compact_kernel(ids_ref, meta_ref, rows_ref, *out_refs, weighted):
    capacity = out_refs[0].shape[1]
    meta = meta_ref[0]
    block = rows_ref[0]
    for k, out_ref in enumerate(out_refs):
        chosen, weight = pick_matrix(ids_ref, meta, k, capacity)
        matrix = jnp.where(chosen, 1.0, 0.0).astype(BF)
        picked = jnp.dot(matrix, block, preferred_element_type=F32)
        if weighted:
            picked = picked * jnp.sum(jnp.where(chosen, weight, 0.0), axis=1, keepdims=True)
        out_ref[0] = picked.astype(BF)


def compact(ids, meta, rows, capacity, weighted):
    blocks, rows_dev, width = rows.shape
    half = width // 2
    return pl.pallas_call(
        functools.partial(compact_kernel, weighted=weighted),
        grid=(blocks, 2),
        in_specs=[
            pl.BlockSpec(memory_space=pltpu.SMEM),
            pl.BlockSpec((1,) + meta.shape[1:], lambda b, h: (b, 0, 0)),
            pl.BlockSpec((1, rows_dev, half), lambda b, h: (b, 0, h)),
        ],
        out_specs=[pl.BlockSpec((1, capacity, half), lambda b, h: (b, 0, h))] * PLANE,
        out_shape=[jax.ShapeDtypeStruct((blocks, capacity, width), BF)] * PLANE,
        name="compact",
    )(ids, meta, rows)


def expand_kernel(ids_ref, meta_ref, *refs, weighted):
    row_refs, out_ref = refs[:PLANE], refs[-1]
    capacity = row_refs[0].shape[1]
    meta = meta_ref[0]
    total = jnp.zeros(out_ref.shape[1:], F32)
    for k, row_ref in enumerate(row_refs):
        chosen, weight = pick_matrix(ids_ref, meta, k, capacity)
        rows = row_ref[0]
        if weighted:
            high = weight.astype(BF).astype(F32)
            parts = [high, weight - high]
        else:
            parts = [1.0]
        for part in parts:
            matrix = jnp.where(chosen, part, 0.0).T.astype(BF)
            total += jnp.dot(matrix, rows, preferred_element_type=F32)
    for extra_ref in refs[PLANE:-1]:
        total += extra_ref[...].astype(F32)
    out_ref[0] = total.astype(BF)


def expand(ids, meta, rows, weighted, extras=()):
    blocks, capacity, width = rows[0].shape
    rows_dev = meta.shape[2]
    half = width // 2
    return pl.pallas_call(
        functools.partial(expand_kernel, weighted=weighted),
        grid=(blocks, 2),
        in_specs=[
            pl.BlockSpec(memory_space=pltpu.SMEM),
            pl.BlockSpec((1,) + meta.shape[1:], lambda b, h: (b, 0, 0)),
        ]
        + [pl.BlockSpec((1, capacity, half), lambda b, h: (b, 0, h))] * PLANE
        + [pl.BlockSpec((rows_dev, half), lambda b, h: (0, h))] * len(extras),
        out_specs=pl.BlockSpec((1, rows_dev, half), lambda b, h: (b, 0, h)),
        out_shape=jax.ShapeDtypeStruct((blocks, rows_dev, width), BF),
        name="expand",
    )(ids, meta, *rows, *extras)


def plane_plan(tokens, routes, gates, cotangent, w_gate, w_up, w_down):
    rows_dev, width = tokens.shape
    picks = routes.shape[1]
    experts = lax.axis_size("expert")
    planes = experts // PLANE
    capacity = rows_dev * picks // experts
    gate_mat, up_mat, down_mat = w_gate[0], w_up[0], w_down[0]
    inner = gate_mat.shape[1]
    here = lax.axis_index("expert")
    level, place = here // PLANE, here % PLANE
    ids = level * PLANE + (place ^ jnp.arange(PLANE, dtype=jnp.int32))
    groups = [[0]] + [sorted({r, planes - r}) for r in range(1, planes // 2 + 1)]

    def rotate(value, turn):
        return lax.ppermute(
            value, "expert", [(i, (i - PLANE * turn) % experts) for i in range(experts)]
        )

    def across(value, bits):
        return lax.ppermute(value, "expert", [(i, i ^ bits) for i in range(experts)])

    def spread(value):
        return {r: value if r == 0 else rotate(value, r) for g in groups for r in g}

    meta_of = spread(jnp.concatenate([routes.astype(F32).T, gates.T], axis=0))
    metas = [jnp.stack([meta_of[r] for r in g]) for g in groups]

    def dispatch(value, weighted):
        block_of = spread(value)
        out = []
        for g, meta in zip(groups, metas):
            rows = compact(ids, meta, jnp.stack([block_of[r] for r in g]), capacity, weighted)
            out.append([rows[0]] + [across(rows[k], k) for k in (3, 1, 2)])
        return out

    def flat(chunks):
        return jnp.concatenate([piece.reshape(-1, width) for chunk in chunks for piece in chunk])

    order = (0, 3, 1, 2)

    def collect(value, weighted):
        start = 0
        pieces = []
        for g in groups:
            count = len(g) * capacity
            chunk = []
            for k in order:
                chunk.append(value[start : start + count].reshape(len(g), capacity, width))
                start += count
            pieces.append(chunk)
        arrived = []
        for at in reversed(range(len(groups))):
            chunk = pieces[at]
            rows = {0: chunk[0]}
            for k, piece in zip(order[1:], chunk[1:]):
                rows[k] = across(piece, k)
            rows = [rows[k] for k in range(PLANE)]
            if at:
                part = expand(ids, metas[at], rows, weighted)
                arrived += [rotate(part[n], -r) for n, r in enumerate(groups[at])]
            else:
                return expand(ids, metas[0], rows, weighted, arrived)[0]

    inputs = flat(dispatch(tokens, False))
    slot_cot = flat(dispatch(cotangent, True))
    gate_pre = jnp.dot(inputs, gate_mat, preferred_element_type=F32)
    up_pre = jnp.dot(inputs, up_mat, preferred_element_type=F32)
    sigma = jax.nn.sigmoid(gate_pre)
    hidden = (gate_pre * sigma * up_pre).astype(BF)
    outputs = jnp.dot(hidden, down_mat, preferred_element_type=F32).astype(BF)
    mixed = collect(outputs, True)
    hidden_grad = jnp.dot(slot_cot, down_mat.T, preferred_element_type=F32)
    gate_grad = (hidden_grad * up_pre * sigma * (1.0 + gate_pre * (1.0 - sigma))).astype(BF)
    up_grad = (hidden_grad * gate_pre * sigma).astype(BF)
    slot_grads = (
        jnp.dot(gate_grad, gate_mat.T, preferred_element_type=F32)
        + jnp.dot(up_grad, up_mat.T, preferred_element_type=F32)
    ).astype(BF)
    input_grad = collect(slot_grads, False)
    down_part = jnp.dot(hidden.T, slot_cot, preferred_element_type=F32)
    gate_part = jnp.dot(inputs.T, gate_grad, preferred_element_type=F32)
    up_part = jnp.dot(inputs.T, up_grad, preferred_element_type=F32)
    return (mixed, input_grad) + relay_sums(gate_part, up_part, down_part)


def on_device(tokens, routes, *rest):
    experts, picks = lax.axis_size("expert"), routes.shape[1]
    if experts % PLANE == 0 and experts <= 2 * picks:
        return plane_plan(tokens, routes, *rest)
    return direct_plan(tokens, routes, *rest)


def solution(mesh):
    rows, stack = P(("pipe", "expert"), None), P("expert", None, None)
    return jax.shard_map(
        on_device,
        mesh=mesh,
        in_specs=(rows, rows, rows, rows, stack, stack, stack),
        out_specs=(rows, rows, stack, stack, stack),
        check_vma=False,
    )
```

```python
import functools

import jax
import jax.numpy as jnp
from jax import lax
from jax.experimental import pallas as pl
from jax.experimental.pallas import tpu as pltpu
from jax.sharding import PartitionSpec as P

PLANE = 4
LEVELS = 4
LAG = 1
BF = jnp.bfloat16
F32 = jnp.float32


def slot_index(block_routes, expert_count, capacity):
    flat = block_routes.reshape(-1)
    onehot = (flat[:, None] == jnp.arange(expert_count, dtype=jnp.int32)[None, :]).astype(jnp.int32)
    before = jnp.cumsum(onehot, axis=0) - onehot
    ranks = jnp.sum(before * onehot, axis=1)
    return flat * capacity + ranks


def expert_forward(block, gate_mat, up_mat, down_mat):
    inputs = block.reshape(-1, block.shape[2])
    gate_pre = jnp.dot(inputs, gate_mat, preferred_element_type=jnp.float32)
    up_pre = jnp.dot(inputs, up_mat, preferred_element_type=jnp.float32)
    sigma = jax.nn.sigmoid(gate_pre)
    hidden = (gate_pre * sigma * up_pre).astype(jnp.bfloat16)
    outputs = jnp.dot(hidden, down_mat, preferred_element_type=jnp.float32).astype(jnp.bfloat16)
    return (gate_pre, up_pre, hidden, outputs)


def direct_plan(tokens, routes, gates, cotangent, w_gate, w_up, w_down):
    rows_dev, width = tokens.shape
    picks = routes.shape[1]
    experts = lax.axis_size("expert")
    capacity = rows_dev * picks // experts
    gate_mat = w_gate[0]
    up_mat = w_up[0]
    down_mat = w_down[0]
    slots = slot_index(routes, experts, capacity)
    flat_rows = jnp.arange(rows_dev * picks, dtype=jnp.int32) // picks
    token_of = jnp.full((experts * capacity,), rows_dev, jnp.int32).at[slots].set(flat_rows)
    weight_of = jnp.zeros((experts * capacity,), jnp.float32).at[slots].set(gates.reshape(-1))
    token_pad = jnp.concatenate([tokens, jnp.zeros((1, width), tokens.dtype)], axis=0)
    send = token_pad[token_of].reshape(experts, capacity, width)

    def exchange(rows):
        return lax.all_to_all(
            rows.reshape(experts, capacity, width), "expert", split_axis=0, concat_axis=0, tiled=True
        )

    block = exchange(send)
    gate_pre, up_pre, hidden, outputs = expert_forward(block, gate_mat, up_mat, down_mat)
    back_items = exchange(outputs)
    inputs = block.reshape(-1, width)
    gathered = back_items.reshape(-1, width)[slots].reshape(rows_dev, picks, width)
    mixed = jnp.sum(gates[:, :, None] * gathered.astype(jnp.float32), axis=1).astype(jnp.bfloat16)
    cot_pad = jnp.concatenate([cotangent, jnp.zeros((1, width), cotangent.dtype)], axis=0)
    cot_send = (weight_of[:, None] * cot_pad[token_of].astype(jnp.float32)).astype(jnp.bfloat16)
    slot_cot = exchange(cot_send).reshape(-1, width)
    down_part = jnp.dot(hidden.T, slot_cot, preferred_element_type=jnp.float32)
    hidden_grad = jnp.dot(slot_cot, down_mat.T, preferred_element_type=jnp.float32)
    sigma = jax.nn.sigmoid(gate_pre)
    gate_grad = (hidden_grad * up_pre * sigma * (1.0 + gate_pre * (1.0 - sigma))).astype(
        jnp.bfloat16
    )
    up_grad = (hidden_grad * gate_pre * sigma).astype(jnp.bfloat16)
    slot_grads = (
        jnp.dot(gate_grad, gate_mat.T, preferred_element_type=jnp.float32)
        + jnp.dot(up_grad, up_mat.T, preferred_element_type=jnp.float32)
    ).astype(jnp.bfloat16)
    grads_back = exchange(slot_grads)
    gate_part = jnp.dot(inputs.T, gate_grad, preferred_element_type=jnp.float32)
    up_part = jnp.dot(inputs.T, up_grad, preferred_element_type=jnp.float32)
    grad_rows = grads_back.reshape(-1, width)[slots].reshape(rows_dev, picks, width)
    input_grad = jnp.sum(grad_rows.astype(jnp.float32), axis=1).astype(jnp.bfloat16)
    return (mixed, input_grad) + relay_sums(gate_part, up_part, down_part)


def relay_sums(*parts):
    relays = lax.axis_size("pipe")
    sums = []
    for part in parts:
        part = part.astype(BF)
        if relays == 2:
            other = lax.ppermute(part, "pipe", [(0, 1), (1, 0)])
            total = (part.astype(F32) + other.astype(F32)).astype(BF)
        else:
            total = lax.psum(part, "pipe")
        sums.append(total[None])
    return tuple(sums)


def chosen_rows(ids_ref, meta, picks, capacity):
    columns = meta.astype(F32).T
    routes, high, low = (columns[n * picks : (n + 1) * picks] for n in range(3))
    rows = meta.shape[0]
    member, weights = [], []
    for k in range(PLANE):
        hit = routes == ids_ref[k].astype(F32)
        member.append(jnp.sum(jnp.where(hit, 1.0, 0.0), axis=0, keepdims=True))
        weights.append(
            [jnp.sum(jnp.where(hit, part, 0.0), axis=0, keepdims=True) for part in (high, low)]
        )
    stacked = jnp.concatenate(member + [jnp.zeros((16 - PLANE, rows), F32)], axis=0)
    first = lax.broadcasted_iota(jnp.int32, (rows, rows), 0)
    second = lax.broadcasted_iota(jnp.int32, (rows, rows), 1)
    ahead = jnp.where(first < second, 1.0, 0.0).astype(BF)
    rank = jnp.dot(stacked.astype(BF), ahead, preferred_element_type=F32)
    slot = lax.broadcasted_iota(jnp.int32, (capacity, rows), 0).astype(F32)
    pick, pick_high, pick_low = [], [], []
    for k in range(PLANE):
        chosen = slot == jnp.where(member[k] > 0.5, rank[k : k + 1], -1.0)
        pick.append(jnp.where(chosen, 1.0, 0.0))
        pick_high.append(jnp.where(chosen, weights[k][0], 0.0))
        pick_low.append(jnp.where(chosen, weights[k][1], 0.0))
    return [jnp.concatenate(part, axis=0) for part in (pick, pick_high, pick_low)]


def put(out_refs, n, start, picked, capacity):
    for k, out_ref in enumerate(out_refs):
        out_ref[n, start : start + capacity] = picked[k * capacity : (k + 1) * capacity]


def picked_rows(matrices, block):
    return sum(jnp.dot(m, block, preferred_element_type=F32) for m in matrices).astype(BF)


def token_kernel(ids_ref, *refs, blocks, halves, cots, picks, capacity):
    meta_refs, refs = refs[: blocks * halves], refs[blocks * halves :]
    row_refs, refs = refs[: blocks * halves], refs[blocks * halves :]
    cot_refs, refs = refs[:cots], refs[cots:]
    table_ref, turned_ref, *out_refs = refs
    for n in range(blocks):
        meta = sum(ref[...] for ref in meta_refs[n * halves : (n + 1) * halves])
        tables = chosen_rows(ids_ref, meta, picks, capacity)
        for m, table in enumerate(tables):
            table_ref[n, m] = table.astype(BF)
            turned_ref[n, m] = table.T.astype(BF)
        block = sum(ref[...] for ref in row_refs[n * halves : (n + 1) * halves])
        put(out_refs, n, 0, picked_rows([table_ref[n, 0]], block), capacity)
        if cots:
            rows = picked_rows([table_ref[n, 1], table_ref[n, 2]], cot_refs[n][...])
            put(out_refs, n, capacity, rows, capacity)


def token_rows(ids, blocks, picks, capacity, width, cots=()):
    halves = len(blocks[0])
    arrays = [a for block in blocks for a in block]
    rows = arrays[0].shape[0]
    count, tall = len(blocks), capacity * (2 if cots else 1)
    spec = [pl.BlockSpec((rows, 128), lambda i: (0, width // 128))] * len(arrays)
    spec += [pl.BlockSpec((rows, width), lambda i: (0, 0))] * (len(arrays) + len(cots))
    shapes = [(count, 3, PLANE * capacity, rows), (count, 3, rows, PLANE * capacity)]
    shapes += [(count, tall, width)] * PLANE
    work = 2 * count * PLANE * capacity * rows * width * (3 if cots else 1)
    moved = 2 * width * (rows * (len(arrays) + len(cots)) + count * PLANE * tall)
    table, turned, *out = pl.pallas_call(
        functools.partial(
            token_kernel, blocks=count, halves=halves, cots=len(cots), picks=picks, capacity=capacity
        ),
        grid=(1,),
        in_specs=[pl.BlockSpec(memory_space=pltpu.SMEM)] + spec,
        out_specs=[pl.BlockSpec(s, lambda i, d=len(s): (0,) * d) for s in shapes],
        out_shape=[jax.ShapeDtypeStruct(s, BF) for s in shapes],
        compiler_params=pltpu.CompilerParams(vmem_limit_bytes=28 << 20),
        cost_estimate=pl.CostEstimate(flops=work, bytes_accessed=moved, transcendentals=0),
        name="token_rows",
    )(ids, *arrays, *arrays, *cots)
    return table, turned, out


def cot_kernel(table_ref, *refs, blocks, halves):
    row_refs, out_refs = refs[: blocks * halves], refs[blocks * halves :]
    capacity = out_refs[0].shape[1]
    for n in range(blocks):
        block = sum(ref[...] for ref in row_refs[n * halves : (n + 1) * halves])
        put(out_refs, n, 0, picked_rows([table_ref[n, 1], table_ref[n, 2]], block), capacity)


def cot_rows(table, blocks):
    halves = len(blocks[0])
    arrays = [a for block in blocks for a in block]
    rows, width = arrays[0].shape
    shape = (len(blocks), table.shape[2] // PLANE, width)
    work = 4 * len(blocks) * table.shape[2] * rows * width
    moved = 2 * width * (rows * len(arrays) + len(blocks) * table.shape[2])
    return pl.pallas_call(
        functools.partial(cot_kernel, blocks=len(blocks), halves=halves),
        out_shape=[jax.ShapeDtypeStruct(shape, BF)] * PLANE,
        compiler_params=pltpu.CompilerParams(vmem_limit_bytes=28 << 20),
        cost_estimate=pl.CostEstimate(flops=work, bytes_accessed=moved, transcendentals=0),
        name="cot_rows",
    )(table, *arrays)


def expand_kernel(turned_ref, *refs, blocks, extras, parts):
    row_refs, extra_refs, out_refs = refs[:PLANE], refs[PLANE:-blocks], refs[-blocks:]
    for n in range(blocks):
        rows = jnp.concatenate([ref[n] for ref in row_refs], axis=0)
        total = sum(jnp.dot(turned_ref[n, m], rows, preferred_element_type=F32) for m in parts)
        for ref in extra_refs[n * extras : (n + 1) * extras]:
            total += ref[...].astype(F32)
        out_refs[n][...] = total.astype(BF)


def expand(turned, rows, weighted, extras):
    blocks, _, width = rows[0].shape
    rows_dev, slots = turned.shape[2:]
    flat = [e for extra in extras for e in extra]
    work = 2 * blocks * rows_dev * slots * width * (2 if weighted else 1)
    moved = 2 * width * (blocks * (slots + rows_dev) + len(flat) * rows_dev)
    return pl.pallas_call(
        functools.partial(
            expand_kernel,
            blocks=blocks,
            extras=len(extras[0]),
            parts=(1, 2) if weighted else (0,),
        ),
        out_shape=[jax.ShapeDtypeStruct((rows_dev, width), BF)] * blocks,
        compiler_params=pltpu.CompilerParams(vmem_limit_bytes=28 << 20),
        cost_estimate=pl.CostEstimate(flops=work, bytes_accessed=moved, transcendentals=0),
        name="expand",
    )(turned, *rows, *flat)


def nt_dot(a, b):
    return lax.dot_general(a, b, (((1,), (1,)), ((), ())), preferred_element_type=F32)


def forward_kernel(*refs, first):
    row_refs, (gate_ref, up_ref, down_ref), refs = refs[:PLANE], refs[PLANE : PLANE + 3], refs[PLANE + 3 :]
    gate_out, up_out, hidden_out, rows_out, *out_refs = refs
    count, capacity, width = out_refs[0].shape
    inputs = jnp.concatenate(
        [ref[n, :capacity] for ref in row_refs for n in range(count)], axis=0
    )
    rows_out[...] = inputs
    gate_pre = jnp.dot(inputs, gate_ref[...], preferred_element_type=F32)
    up_pre = jnp.dot(inputs, up_ref[...], preferred_element_type=F32)
    gate_out[...] = gate_pre
    up_out[...] = up_pre
    hidden = (gate_pre * jax.nn.sigmoid(gate_pre) * up_pre).astype(BF)
    hidden_out[...] = hidden
    outputs = jnp.dot(hidden, down_ref[...], preferred_element_type=F32).astype(BF)
    for k, out_ref in enumerate(out_refs):
        for n in range(count):
            at = (k * count + n) * capacity
            out_ref[n] = outputs[at : at + capacity]


def forward(rows, capacity, gate_mat, up_mat, down_mat):
    count, _, width = rows[0].shape
    inner = gate_mat.shape[1]
    total = PLANE * count * capacity
    return pl.pallas_call(
        functools.partial(forward_kernel, first=capacity),
        out_shape=[
            jax.ShapeDtypeStruct((total, inner), F32),
            jax.ShapeDtypeStruct((total, inner), F32),
            jax.ShapeDtypeStruct((total, inner), BF),
            jax.ShapeDtypeStruct((total, width), BF),
        ]
        + [jax.ShapeDtypeStruct((count, capacity, width), BF)] * PLANE,
        compiler_params=pltpu.CompilerParams(vmem_limit_bytes=36 << 20),
        cost_estimate=pl.CostEstimate(
            flops=6 * total * width * inner,
            bytes_accessed=6 * width * inner + 6 * total * width + 10 * total * inner,
            transcendentals=total * inner,
        ),
        name="expert_forward",
    )(*rows, gate_mat, up_mat, down_mat)


def backward_kernel(*refs, skip):
    cot_refs, refs = refs[:PLANE], refs[PLANE:]
    gate_pre_ref, up_pre_ref, gate_ref, up_ref, down_ref, *refs = refs
    gate_out, up_out, rows_out, *out_refs = refs
    count, capacity, width = out_refs[0].shape
    cots = jnp.concatenate(
        [ref[n, skip : skip + capacity] for ref in cot_refs for n in range(count)], axis=0
    )
    rows_out[...] = cots
    hidden_grad = nt_dot(cots, down_ref[...])
    gate_pre, up_pre = gate_pre_ref[...], up_pre_ref[...]
    sigma = jax.nn.sigmoid(gate_pre)
    gate_grad = (hidden_grad * up_pre * sigma * (1.0 + gate_pre * (1.0 - sigma))).astype(BF)
    up_grad = (hidden_grad * gate_pre * sigma).astype(BF)
    gate_out[...] = gate_grad
    up_out[...] = up_grad
    grads = (nt_dot(gate_grad, gate_ref[...]) + nt_dot(up_grad, up_ref[...])).astype(BF)
    for k, out_ref in enumerate(out_refs):
        for n in range(count):
            at = (k * count + n) * capacity
            out_ref[n] = grads[at : at + capacity]


def backward(cots, skip, capacity, gate_pre, up_pre, gate_mat, up_mat, down_mat):
    count, _, width = cots[0].shape
    total, inner = gate_pre.shape
    return pl.pallas_call(
        functools.partial(backward_kernel, skip=skip),
        out_shape=[
            jax.ShapeDtypeStruct((total, inner), BF),
            jax.ShapeDtypeStruct((total, inner), BF),
            jax.ShapeDtypeStruct((total, width), BF),
        ]
        + [jax.ShapeDtypeStruct((count, capacity, width), BF)] * PLANE,
        compiler_params=pltpu.CompilerParams(vmem_limit_bytes=36 << 20),
        cost_estimate=pl.CostEstimate(
            flops=6 * total * width * inner,
            bytes_accessed=6 * width * inner + 6 * total * width + 12 * total * inner,
            transcendentals=total * inner,
        ),
        name="expert_backward",
    )(*cots, gate_pre, up_pre, gate_mat, up_mat, down_mat)


def plane_plan(tokens, routes, gates, cotangent, w_gate, w_up, w_down):
    rows_dev, width = tokens.shape
    picks = routes.shape[1]
    experts = lax.axis_size("expert")
    capacity = rows_dev * picks // experts
    mats = (w_gate[0], w_up[0], w_down[0])
    here = lax.axis_index("expert")
    level, place = here // PLANE, here % PLANE
    ids = level * PLANE + (place ^ jnp.arange(PLANE, dtype=jnp.int32))

    def shift(value, levels, step):
        pairs = [
            (level * PLANE + p, (level + step) % LEVELS * PLANE + p)
            for level in levels
            for p in range(PLANE)
        ]
        return lax.ppermute(value, "expert", pairs)

    stages = []

    def across(rows):
        sent = tuple(rows[1:])
        if len(stages) >= LAG:
            sent, _ = lax.optimization_barrier((sent, stages[-LAG]))
        moved = {
            k: lax.ppermute(sent[k - 1], "expert", [(i, i ^ k) for i in range(experts)])
            for k in (3, 1, 2)
        }
        stages.append(tuple(moved[k] for k in range(1, PLANE)))
        return [rows[0], *stages[-1]]

    every = range(LEVELS)
    high = lax.reduce_precision(gates, 8, 7)
    low = lax.reduce_precision(gates - high, 8, 7)
    meta = jnp.concatenate([routes.astype(F32), high, low], axis=1).astype(BF)
    meta = jnp.pad(meta, ((0, 0), (0, 128 - meta.shape[1])))
    block = jnp.concatenate([tokens, meta], axis=1)

    def pick(blocks, cots=()):
        return token_rows(ids, blocks, picks, capacity, width, cots)

    above, below = shift(block, every, -1), shift(block, every, 1)
    table_a, turned_a, rows_a = pick([[block]], [cotangent])
    rows_a = across(rows_a)
    far = [shift(above, (1, 2), -1), shift(below, (1, 2), 1)]
    table_b, turned_b, rows_b = pick([[above], [below]])
    rows_b = across(rows_b)
    later, far = lax.optimization_barrier((cotangent, far))
    cot_above, cot_below = shift(later, every, -1), shift(later, every, 1)
    table_c, turned_c, rows_c = pick([far])
    rows_c = across(rows_c)
    cot_far = [shift(cot_above, (1, 2), -1), shift(cot_below, (1, 2), 1)]
    cots_b = across(cot_rows(table_b, [[cot_above], [cot_below]]))
    cots_c = across(cot_rows(table_c, [cot_far]))

    saved, outs = [], []
    for rows in (rows_a, rows_b, rows_c):
        gate_pre, up_pre, hidden, inputs, *out = forward(rows, capacity, *mats)
        saved.append((gate_pre, up_pre, hidden, inputs))
        outs.append(out)
    grads, grad_outs = [], []
    for cots, skip, (gate_pre, up_pre, _, _) in zip(
        (rows_a, cots_b, cots_c), (capacity, 0, 0), saved
    ):
        gate_grad, up_grad, flat, *out = backward(cots, skip, capacity, gate_pre, up_pre, *mats)
        grads.append((gate_grad, up_grad, flat))
        grad_outs.append(out)

    flows = ((outs, True), (grad_outs, False))
    relayed = []
    for rows, weighted in flows:
        (part,) = expand(turned_c, across(rows[2]), weighted, [[]])
        relayed.append((shift(part, (0, 1), 1), shift(part, (3, 2), -1)))
    arrived = []
    for (rows, weighted), (up, down) in zip(flows, relayed):
        near = expand(turned_b, across(rows[1]), weighted, [[up], [down]])
        arrived.append([shift(near[0], every, 1), shift(near[1], every, -1)])
    mixed, input_grad = (
        expand(turned_a, across(rows[0]), weighted, [extra])[0]
        for (rows, weighted), extra in zip(flows, arrived)
    )
    hidden, inputs = (jnp.concatenate([s[n] for s in saved]) for n in (2, 3))
    gate_grad, up_grad, slot_cot = (jnp.concatenate([g[n] for g in grads]) for n in range(3))
    down_part = jnp.dot(hidden.T, slot_cot, preferred_element_type=F32)
    gate_part = jnp.dot(inputs.T, gate_grad, preferred_element_type=F32)
    up_part = jnp.dot(inputs.T, up_grad, preferred_element_type=F32)
    return (mixed, input_grad) + relay_sums(gate_part, up_part, down_part)


def on_device(tokens, routes, *rest):
    experts, picks = lax.axis_size("expert"), routes.shape[1]
    if experts == LEVELS * PLANE and experts <= 2 * picks:
        return plane_plan(tokens, routes, *rest)
    return direct_plan(tokens, routes, *rest)


def solution(mesh):
    rows, stack = P(("pipe", "expert"), None), P("expert", None, None)
    return jax.shard_map(
        on_device,
        mesh=mesh,
        in_specs=(rows, rows, rows, rows, stack, stack, stack),
        out_specs=(rows, rows, stack, stack, stack),
        check_vma=False,
    )
```

```python
import functools

import jax
import jax.numpy as jnp
from jax import lax
from jax.experimental import pallas as pl
from jax.experimental.pallas import tpu as pltpu
from jax.sharding import PartitionSpec as P

PLANE = 4
LEVELS = 4
BF = jnp.bfloat16
F32 = jnp.float32


def slot_index(block_routes, expert_count, capacity):
    flat = block_routes.reshape(-1)
    onehot = (flat[:, None] == jnp.arange(expert_count, dtype=jnp.int32)[None, :]).astype(jnp.int32)
    before = jnp.cumsum(onehot, axis=0) - onehot
    ranks = jnp.sum(before * onehot, axis=1)
    return flat * capacity + ranks


def expert_forward(block, gate_mat, up_mat, down_mat):
    inputs = block.reshape(-1, block.shape[2])
    gate_pre = jnp.dot(inputs, gate_mat, preferred_element_type=jnp.float32)
    up_pre = jnp.dot(inputs, up_mat, preferred_element_type=jnp.float32)
    sigma = jax.nn.sigmoid(gate_pre)
    hidden = (gate_pre * sigma * up_pre).astype(jnp.bfloat16)
    outputs = jnp.dot(hidden, down_mat, preferred_element_type=jnp.float32).astype(jnp.bfloat16)
    return (gate_pre, up_pre, hidden, outputs)


def direct_plan(tokens, routes, gates, cotangent, w_gate, w_up, w_down):
    rows_dev, width = tokens.shape
    picks = routes.shape[1]
    experts = lax.axis_size("expert")
    capacity = rows_dev * picks // experts
    gate_mat = w_gate[0]
    up_mat = w_up[0]
    down_mat = w_down[0]
    slots = slot_index(routes, experts, capacity)
    flat_rows = jnp.arange(rows_dev * picks, dtype=jnp.int32) // picks
    token_of = jnp.full((experts * capacity,), rows_dev, jnp.int32).at[slots].set(flat_rows)
    weight_of = jnp.zeros((experts * capacity,), jnp.float32).at[slots].set(gates.reshape(-1))
    token_pad = jnp.concatenate([tokens, jnp.zeros((1, width), tokens.dtype)], axis=0)
    send = token_pad[token_of].reshape(experts, capacity, width)

    def exchange(rows):
        return lax.all_to_all(
            rows.reshape(experts, capacity, width), "expert", split_axis=0, concat_axis=0, tiled=True
        )

    block = exchange(send)
    gate_pre, up_pre, hidden, outputs = expert_forward(block, gate_mat, up_mat, down_mat)
    back_items = exchange(outputs)
    inputs = block.reshape(-1, width)
    gathered = back_items.reshape(-1, width)[slots].reshape(rows_dev, picks, width)
    mixed = jnp.sum(gates[:, :, None] * gathered.astype(jnp.float32), axis=1).astype(jnp.bfloat16)
    cot_pad = jnp.concatenate([cotangent, jnp.zeros((1, width), cotangent.dtype)], axis=0)
    cot_send = (weight_of[:, None] * cot_pad[token_of].astype(jnp.float32)).astype(jnp.bfloat16)
    slot_cot = exchange(cot_send).reshape(-1, width)
    down_part = jnp.dot(hidden.T, slot_cot, preferred_element_type=jnp.float32)
    hidden_grad = jnp.dot(slot_cot, down_mat.T, preferred_element_type=jnp.float32)
    sigma = jax.nn.sigmoid(gate_pre)
    gate_grad = (hidden_grad * up_pre * sigma * (1.0 + gate_pre * (1.0 - sigma))).astype(
        jnp.bfloat16
    )
    up_grad = (hidden_grad * gate_pre * sigma).astype(jnp.bfloat16)
    slot_grads = (
        jnp.dot(gate_grad, gate_mat.T, preferred_element_type=jnp.float32)
        + jnp.dot(up_grad, up_mat.T, preferred_element_type=jnp.float32)
    ).astype(jnp.bfloat16)
    grads_back = exchange(slot_grads)
    gate_part = jnp.dot(inputs.T, gate_grad, preferred_element_type=jnp.float32)
    up_part = jnp.dot(inputs.T, up_grad, preferred_element_type=jnp.float32)
    grad_rows = grads_back.reshape(-1, width)[slots].reshape(rows_dev, picks, width)
    input_grad = jnp.sum(grad_rows.astype(jnp.float32), axis=1).astype(jnp.bfloat16)
    return (mixed, input_grad) + relay_sums(gate_part, up_part, down_part)


def relay_sums(*parts):
    relays = lax.axis_size("pipe")
    sums = []
    for part in parts:
        part = part.astype(BF)
        if relays == 2:
            other = lax.ppermute(part, "pipe", [(0, 1), (1, 0)])
            total = (part.astype(F32) + other.astype(F32)).astype(BF)
        else:
            total = lax.psum(part, "pipe")
        sums.append(total[None])
    return tuple(sums)


def chosen_rows(ids_ref, meta, picks, capacity):
    columns = meta.T
    routes, high, low = (columns[n * picks : (n + 1) * picks] for n in range(3))
    rows = meta.shape[0]
    member, weights = [], []
    for k in range(PLANE):
        hit = routes == ids_ref[k].astype(F32)
        member.append(jnp.sum(jnp.where(hit, 1.0, 0.0), axis=0, keepdims=True))
        weights.append(
            [jnp.sum(jnp.where(hit, part, 0.0), axis=0, keepdims=True) for part in (high, low)]
        )
    stacked = jnp.concatenate(member + [jnp.zeros((16 - PLANE, rows), F32)], axis=0)
    first = lax.broadcasted_iota(jnp.int32, (rows, rows), 0)
    second = lax.broadcasted_iota(jnp.int32, (rows, rows), 1)
    ahead = jnp.where(first < second, 1.0, 0.0).astype(BF)
    rank = jnp.dot(stacked.astype(BF), ahead, preferred_element_type=F32)
    slot = lax.broadcasted_iota(jnp.int32, (capacity, rows), 0).astype(F32)
    pick, pick_high, pick_low = [], [], []
    for k in range(PLANE):
        chosen = slot == jnp.where(member[k] > 0.5, rank[k : k + 1], -1.0)
        pick.append(jnp.where(chosen, 1.0, 0.0))
        pick_high.append(jnp.where(chosen, weights[k][0], 0.0))
        pick_low.append(jnp.where(chosen, weights[k][1], 0.0))
    return [jnp.concatenate(part, axis=0) for part in (pick, pick_high, pick_low)]


def put(out_refs, n, start, picked, capacity):
    for k, out_ref in enumerate(out_refs):
        out_ref[n, start : start + capacity] = picked[k * capacity : (k + 1) * capacity]


def picked_rows(matrices, block):
    return sum(jnp.dot(m, block, preferred_element_type=F32) for m in matrices).astype(BF)


def start_kernel(ids_ref, tokens_ref, routes_ref, gates_ref, cot_ref, block_ref, *refs, picks, capacity):
    table_ref, turned_ref, *out_refs = refs
    rows, width = tokens_ref.shape
    gates = gates_ref[...]
    high = gates.astype(BF)
    low = (gates - high.astype(F32)).astype(BF)
    lane = lax.broadcasted_iota(jnp.int32, (picks, 128), 1)
    row = lax.broadcasted_iota(jnp.int32, (picks, 128), 0)
    meta = jnp.zeros((rows, 128), F32)
    for n, part in enumerate((routes_ref[...].astype(F32).astype(BF), high, low)):
        place = jnp.where(lane == row + n * picks, 1.0, 0.0).astype(BF)
        meta += jnp.dot(part, place, preferred_element_type=F32)
    block_ref[:, :width] = tokens_ref[...]
    block_ref[:, width:] = meta.astype(BF)
    write_tables(ids_ref, meta, table_ref, turned_ref, 0, picks, capacity)
    put(out_refs, 0, 0, picked_rows([table_ref[0, 0]], tokens_ref[...]), capacity)
    rows = picked_rows([table_ref[0, 1], table_ref[0, 2]], cot_ref[...])
    put(out_refs, 0, capacity, rows, capacity)


def write_tables(ids_ref, meta, table_ref, turned_ref, n, picks, capacity):
    for m, table in enumerate(chosen_rows(ids_ref, meta, picks, capacity)):
        table_ref[n, m] = table.astype(BF)
        turned_ref[n, m] = table.T.astype(BF)


def table_shapes(count, capacity, rows):
    return [(count, 3, PLANE * capacity, rows), (count, 3, rows, PLANE * capacity)]


def start_rows(ids, tokens, routes, gates, cotangent, capacity):
    rows, width = tokens.shape
    picks = routes.shape[1]
    shapes = [(rows, width + 128)] + table_shapes(1, capacity, rows)
    shapes += [(1, 2 * capacity, width)] * PLANE
    block, table, turned, *out = pl.pallas_call(
        functools.partial(start_kernel, picks=picks, capacity=capacity),
        in_specs=[pl.BlockSpec(memory_space=pltpu.SMEM)]
        + [pl.BlockSpec(memory_space=pltpu.VMEM)] * 4,
        out_shape=[jax.ShapeDtypeStruct(s, BF) for s in shapes],
        compiler_params=pltpu.CompilerParams(vmem_limit_bytes=28 << 20),
        name="start_rows",
    )(ids, tokens, routes, gates, cotangent)
    return block, table, turned, out


def token_kernel(ids_ref, *refs, blocks, picks, capacity):
    meta_refs, row_refs, refs = refs[:blocks], refs[blocks : 2 * blocks], refs[2 * blocks :]
    table_ref, turned_ref, *out_refs = refs
    if blocks == 2:
        *out_refs, pass_ref = out_refs
        width = row_refs[0].shape[1]
        first = ids_ref[PLANE] == 1
        pass_ref[:, :width] = jnp.where(first, row_refs[0][...], row_refs[1][...])
        pass_ref[:, width:] = jnp.where(first, meta_refs[0][...], meta_refs[1][...])
    for n in range(blocks):
        meta = meta_refs[n][...].astype(F32)
        write_tables(ids_ref, meta, table_ref, turned_ref, n, picks, capacity)
        put(out_refs, n, 0, picked_rows([table_ref[n, 0]], row_refs[n][...]), capacity)


def token_rows(ids, blocks, picks, capacity):
    rows, wide = blocks[0].shape
    width, count = wide - 128, len(blocks)
    spec = [pl.BlockSpec((rows, 128), lambda i: (0, width // 128))] * count
    spec += [pl.BlockSpec((rows, width), lambda i: (0, 0))] * count
    shapes = table_shapes(count, capacity, rows) + [(count, capacity, width)] * PLANE
    if count == 2:
        shapes.append((rows, wide))
    table, turned, *out = pl.pallas_call(
        functools.partial(token_kernel, blocks=count, picks=picks, capacity=capacity),
        grid=(1,),
        in_specs=[pl.BlockSpec(memory_space=pltpu.SMEM)] + spec,
        out_specs=[pl.BlockSpec(s, lambda i, d=len(s): (0,) * d) for s in shapes],
        out_shape=[jax.ShapeDtypeStruct(s, BF) for s in shapes],
        compiler_params=pltpu.CompilerParams(vmem_limit_bytes=28 << 20),
        name="token_rows",
    )(ids, *blocks, *blocks)
    return table, turned, out


def cot_kernel(ids_ref, table_ref, *refs, blocks):
    row_refs, out_refs = refs[:blocks], refs[blocks:]
    if blocks == 2:
        *out_refs, pass_ref = out_refs
        pass_ref[...] = jnp.where(ids_ref[PLANE] == 1, row_refs[0][...], row_refs[1][...])
    for n in range(blocks):
        rows = picked_rows([table_ref[n, 1], table_ref[n, 2]], row_refs[n][...])
        put(out_refs, n, 0, rows, out_refs[0].shape[1])


def cot_rows(ids, table, blocks):
    rows, width = blocks[0].shape
    shapes = [(len(blocks), table.shape[2] // PLANE, width)] * PLANE
    if len(blocks) == 2:
        shapes.append((rows, width))
    return pl.pallas_call(
        functools.partial(cot_kernel, blocks=len(blocks)),
        in_specs=[pl.BlockSpec(memory_space=pltpu.SMEM)]
        + [pl.BlockSpec(memory_space=pltpu.VMEM)] * (1 + len(blocks)),
        out_shape=[jax.ShapeDtypeStruct(s, BF) for s in shapes],
        compiler_params=pltpu.CompilerParams(vmem_limit_bytes=28 << 20),
        name="cot_rows",
    )(ids, table, *blocks)


def expand_kernel(flags_ref, turned_ref, *refs, blocks, extras, parts, flagged):
    row_refs, extra_refs, out_refs = refs[:PLANE], refs[PLANE : PLANE + extras], refs[-blocks:]
    for n in range(blocks):
        rows = jnp.concatenate([ref[n] for ref in row_refs], axis=0)
        total = sum(jnp.dot(turned_ref[n, m], rows, preferred_element_type=F32) for m in parts)
        for ref in extra_refs:
            extra = ref[...].astype(F32)
            total += jnp.where(flags_ref[n] == 1, extra, 0.0) if flagged else extra
        out_refs[n][...] = total.astype(BF)


def expand(turned, rows, weighted, extras=(), flags=None):
    blocks, _, width = rows[0].shape
    rows_dev, slots = turned.shape[2:]
    work = 2 * blocks * rows_dev * slots * width * (2 if weighted else 1)
    moved = 2 * width * (blocks * (slots + rows_dev) + len(extras) * rows_dev)
    return pl.pallas_call(
        functools.partial(
            expand_kernel,
            blocks=blocks,
            extras=len(extras),
            parts=(1, 2) if weighted else (0,),
            flagged=flags is not None,
        ),
        in_specs=[pl.BlockSpec(memory_space=pltpu.SMEM)]
        + [pl.BlockSpec(memory_space=pltpu.VMEM)] * (1 + len(rows) + len(extras)),
        out_shape=[jax.ShapeDtypeStruct((rows_dev, width), BF)] * blocks,
        compiler_params=pltpu.CompilerParams(vmem_limit_bytes=28 << 20),
        cost_estimate=pl.CostEstimate(flops=work, bytes_accessed=moved, transcendentals=0),
        name="expand",
    )(jnp.zeros((2,), jnp.int32) if flags is None else flags, turned, *rows, *extras)


def nt_dot(a, b):
    return lax.dot_general(a, b, (((1,), (1,)), ((), ())), preferred_element_type=F32)


def forward_kernel(*refs, first):
    row_refs, (gate_ref, up_ref, down_ref), refs = refs[:PLANE], refs[PLANE : PLANE + 3], refs[PLANE + 3 :]
    gate_out, up_out, hidden_out, rows_out, *out_refs = refs
    count, capacity, width = out_refs[0].shape
    inputs = jnp.concatenate(
        [ref[n, :capacity] for ref in row_refs for n in range(count)], axis=0
    )
    rows_out[...] = inputs
    gate_pre = jnp.dot(inputs, gate_ref[...], preferred_element_type=F32)
    up_pre = jnp.dot(inputs, up_ref[...], preferred_element_type=F32)
    gate_out[...] = gate_pre
    up_out[...] = up_pre
    hidden = (gate_pre * jax.nn.sigmoid(gate_pre) * up_pre).astype(BF)
    hidden_out[...] = hidden.astype(F32).T.astype(BF)
    outputs = jnp.dot(hidden, down_ref[...], preferred_element_type=F32).astype(BF)
    for k, out_ref in enumerate(out_refs):
        for n in range(count):
            at = (k * count + n) * capacity
            out_ref[n] = outputs[at : at + capacity]


def forward(rows, capacity, gate_mat, up_mat, down_mat):
    count, _, width = rows[0].shape
    inner = gate_mat.shape[1]
    total = PLANE * count * capacity
    return pl.pallas_call(
        functools.partial(forward_kernel, first=capacity),
        out_shape=[
            jax.ShapeDtypeStruct((total, inner), F32),
            jax.ShapeDtypeStruct((total, inner), F32),
            jax.ShapeDtypeStruct((inner, total), BF),
            jax.ShapeDtypeStruct((total, width), BF),
        ]
        + [jax.ShapeDtypeStruct((count, capacity, width), BF)] * PLANE,
        compiler_params=pltpu.CompilerParams(vmem_limit_bytes=36 << 20),
        cost_estimate=pl.CostEstimate(
            flops=6 * total * width * inner,
            bytes_accessed=6 * width * inner + 6 * total * width + 10 * total * inner,
            transcendentals=total * inner,
        ),
        name="expert_forward",
    )(*rows, gate_mat, up_mat, down_mat)


def backward_kernel(*refs, skip):
    cot_refs, refs = refs[:PLANE], refs[PLANE:]
    gate_pre_ref, up_pre_ref, gate_ref, up_ref, down_ref, *refs = refs
    gate_out, up_out, rows_out, *out_refs = refs
    count, capacity, width = out_refs[0].shape
    cots = jnp.concatenate(
        [ref[n, skip : skip + capacity] for ref in cot_refs for n in range(count)], axis=0
    )
    rows_out[...] = cots
    hidden_grad = nt_dot(cots, down_ref[...])
    gate_pre, up_pre = gate_pre_ref[...], up_pre_ref[...]
    sigma = jax.nn.sigmoid(gate_pre)
    gate_grad = (hidden_grad * up_pre * sigma * (1.0 + gate_pre * (1.0 - sigma))).astype(BF)
    up_grad = (hidden_grad * gate_pre * sigma).astype(BF)
    gate_out[...] = gate_grad.astype(F32).T.astype(BF)
    up_out[...] = up_grad.astype(F32).T.astype(BF)
    grads = (nt_dot(gate_grad, gate_ref[...]) + nt_dot(up_grad, up_ref[...])).astype(BF)
    for k, out_ref in enumerate(out_refs):
        for n in range(count):
            at = (k * count + n) * capacity
            out_ref[n] = grads[at : at + capacity]


def backward(cots, skip, capacity, gate_pre, up_pre, gate_mat, up_mat, down_mat):
    count, _, width = cots[0].shape
    total, inner = gate_pre.shape
    return pl.pallas_call(
        functools.partial(backward_kernel, skip=skip),
        out_shape=[
            jax.ShapeDtypeStruct((inner, total), BF),
            jax.ShapeDtypeStruct((inner, total), BF),
            jax.ShapeDtypeStruct((total, width), BF),
        ]
        + [jax.ShapeDtypeStruct((count, capacity, width), BF)] * PLANE,
        compiler_params=pltpu.CompilerParams(vmem_limit_bytes=36 << 20),
        cost_estimate=pl.CostEstimate(
            flops=6 * total * width * inner,
            bytes_accessed=6 * width * inner + 6 * total * width + 12 * total * inner,
            transcendentals=total * inner,
        ),
        name="expert_backward",
    )(*cots, gate_pre, up_pre, gate_mat, up_mat, down_mat)


def partial_kernel(*refs):
    out_ref = refs[-1]
    chunks = (len(refs) - 1) // 5
    hidden, gate_grad, up_grad, inputs, cots = (
        refs[n * chunks : (n + 1) * chunks] for n in range(5)
    )
    for n, (left, right) in enumerate(((gate_grad, inputs), (up_grad, inputs), (hidden, cots))):
        total = sum(
            jnp.dot(a[...], b[...], preferred_element_type=F32) for a, b in zip(left, right)
        )
        out_ref[n] = total.astype(BF)


def partial_sums(hidden, gate_grad, up_grad, inputs, cots):
    inner, width = hidden[0].shape[0], inputs[0].shape[1]
    total = sum(a.shape[0] for a in inputs)
    tile = min(512, width)
    small = [*hidden, *gate_grad, *up_grad]
    large = [*inputs, *cots]
    return pl.pallas_call(
        partial_kernel,
        grid=(width // tile,),
        in_specs=[pl.BlockSpec(a.shape, lambda i: (0, 0)) for a in small]
        + [pl.BlockSpec((a.shape[0], tile), lambda i: (0, i)) for a in large],
        out_specs=pl.BlockSpec((3, inner, tile), lambda i: (0, 0, i)),
        out_shape=jax.ShapeDtypeStruct((3, inner, width), BF),
        compiler_params=pltpu.CompilerParams(vmem_limit_bytes=36 << 20),
        cost_estimate=pl.CostEstimate(
            flops=6 * total * inner * width,
            bytes_accessed=6 * total * inner + 4 * total * width + 6 * inner * width,
            transcendentals=0,
        ),
        name="partial_sums",
    )(*small, *large)


def turn_kernel(*refs):
    *sum_refs, gate_ref, up_ref, down_ref = refs
    for n, out_ref in enumerate((gate_ref, up_ref, down_ref)):
        total = sum(ref[n].astype(F32) for ref in sum_refs)
        out_ref[0] = (total if n == 2 else total.T).astype(BF)


def weight_outputs(*sums):
    _, inner, width = sums[0].shape
    tile = min(512, width)
    return pl.pallas_call(
        turn_kernel,
        grid=(width // tile,),
        in_specs=[pl.BlockSpec((3, inner, tile), lambda i: (0, 0, i))] * len(sums),
        out_specs=[
            pl.BlockSpec((1, tile, inner), lambda i: (0, i, 0)),
            pl.BlockSpec((1, tile, inner), lambda i: (0, i, 0)),
            pl.BlockSpec((1, inner, tile), lambda i: (0, 0, i)),
        ],
        out_shape=[
            jax.ShapeDtypeStruct((1, width, inner), BF),
            jax.ShapeDtypeStruct((1, width, inner), BF),
            jax.ShapeDtypeStruct((1, inner, width), BF),
        ],
        compiler_params=pltpu.CompilerParams(vmem_limit_bytes=28 << 20),
        cost_estimate=pl.CostEstimate(
            flops=6 * inner * width,
            bytes_accessed=6 * inner * width * (1 + len(sums)),
            transcendentals=0,
        ),
        name="weight_outputs",
    )(*sums)


def plane_plan(tokens, routes, gates, cotangent, w_gate, w_up, w_down):
    rows_dev, width = tokens.shape
    picks = routes.shape[1]
    experts = lax.axis_size("expert")
    capacity = rows_dev * picks // experts
    mats = (w_gate[0], w_up[0], w_down[0])
    here = lax.axis_index("expert")
    level, place = here // PLANE, here % PLANE
    odd = level % 2
    ids = jnp.stack([level * PLANE + (place ^ k) for k in range(PLANE)] + [odd])

    def permute(value, step):
        pairs = [(i, step(i // PLANE) % LEVELS * PLANE + i % PLANE) for i in range(experts)]
        return lax.ppermute(value, "expert", pairs)

    def from_above(value):
        return permute(value, lambda n: n - 1)

    def from_below(value):
        return permute(value, lambda n: n + 1)

    def swap(value):
        return permute(value, lambda n: n ^ 1)

    stages = []

    def across(rows, *deps):
        sent = tuple(rows[1:])
        if stages or deps:
            sent, *_ = lax.optimization_barrier((sent, *stages[-1:], *deps))
        moved = {
            k: lax.ppermute(sent[k - 1], "expert", [(i, i ^ k) for i in range(experts)])
            for k in (3, 1, 2)
        }
        stages.append(tuple(moved[k] for k in range(1, PLANE)))
        return [rows[0], *stages[-1]]

    block, table_a, turned_a, rows_a = start_rows(ids, tokens, routes, gates, cotangent, capacity)
    rows_a = across(rows_a)
    above, below = from_above(block), from_below(block)
    table_b, turned_b, (*rows_b, far) = token_rows(ids, [above, below], picks, capacity)
    far = swap(far)
    rows_b = across(rows_b)
    later, far = lax.optimization_barrier((cotangent, far))
    cot_above, cot_below = from_above(later), from_below(later)
    table_c, turned_c, rows_c = token_rows(ids, [far], picks, capacity)
    rows_c = across(rows_c)
    *cots_b, cot_far = cot_rows(ids, table_b, [cot_above, cot_below])
    cot_far = swap(cot_far)
    cots_b = across(cots_b)

    saved = [forward(rows, capacity, *mats) for rows in (rows_a, rows_b, rows_c)]
    outs = [s[4:] for s in saved]

    def back(cots, skip, forth):
        return backward(cots, skip, capacity, forth[0], forth[1], *mats)

    back_a = back(rows_a, capacity, saved[0])
    cots_c = across(cot_rows(ids, table_c, [cot_far]), saved, back_a)
    back_b = back(cots_b, 0, saved[1])
    mixed_c = across(outs[2], back_b)
    back_c = back(cots_c, 0, saved[2])
    backs = (back_a, back_b, back_c)
    partial = partial_sums(
        [s[2] for s in saved],
        [b[0] for b in backs],
        [b[1] for b in backs],
        [s[3] for s in saved],
        [b[2] for b in backs],
    )
    grads_c = across(back_c[3:], partial)
    passed = jnp.stack([odd, 1 - odd])

    def send_near(rows, weighted, far, *deps):
        near = expand(turned_b, rows, weighted, [far], passed)
        near, *_ = lax.optimization_barrier((near, *deps))
        return from_below(near[0]), from_above(near[1])

    mixed_far = swap(*expand(turned_c, mixed_c, True))
    sent, _ = lax.optimization_barrier((partial, mixed_c))
    other = lax.ppermute(sent, "pipe", [(0, 1), (1, 0)])
    mixed_b = across(outs[1])
    grads_far = swap(*expand(turned_c, grads_c, False))
    weight_grads = weight_outputs(partial, other)
    grads_b = across(back_b[3:], mixed_far, grads_far, weight_grads)
    mixed_near = send_near(mixed_b, True, mixed_far, grads_far)
    mixed_a = across(outs[0])
    grads_near = send_near(grads_b, False, grads_far, mixed_near)
    grads_a = across(back_a[3:], mixed_near)
    mixed = expand(turned_a, mixed_a, True, mixed_near)
    input_grad = expand(turned_a, grads_a, False, grads_near)
    return (*mixed, *input_grad, *weight_grads)


def on_device(tokens, routes, *rest):
    experts, picks = lax.axis_size("expert"), routes.shape[1]
    if experts == LEVELS * PLANE and lax.axis_size("pipe") == 2 and experts <= 2 * picks:
        return plane_plan(tokens, routes, *rest)
    return direct_plan(tokens, routes, *rest)


def solution(mesh):
    rows, stack = P(("pipe", "expert"), None), P("expert", None, None)
    return jax.shard_map(
        on_device,
        mesh=mesh,
        in_specs=(rows, rows, rows, rows, stack, stack, stack),
        out_specs=(rows, rows, stack, stack, stack),
        check_vma=False,
    )
```

```python
import functools

import jax
import jax.numpy as jnp
from jax import lax
from jax.experimental import pallas as pl
from jax.experimental.pallas import tpu as pltpu
from jax.sharding import PartitionSpec as P

PLANE = 4
LEVELS = 4
BF = jnp.bfloat16
F32 = jnp.float32


def slot_index(block_routes, expert_count, capacity):
    flat = block_routes.reshape(-1)
    onehot = (flat[:, None] == jnp.arange(expert_count, dtype=jnp.int32)[None, :]).astype(jnp.int32)
    before = jnp.cumsum(onehot, axis=0) - onehot
    ranks = jnp.sum(before * onehot, axis=1)
    return flat * capacity + ranks


def expert_forward(block, gate_mat, up_mat, down_mat):
    inputs = block.reshape(-1, block.shape[2])
    gate_pre = jnp.dot(inputs, gate_mat, preferred_element_type=jnp.float32)
    up_pre = jnp.dot(inputs, up_mat, preferred_element_type=jnp.float32)
    sigma = jax.nn.sigmoid(gate_pre)
    hidden = (gate_pre * sigma * up_pre).astype(jnp.bfloat16)
    outputs = jnp.dot(hidden, down_mat, preferred_element_type=jnp.float32).astype(jnp.bfloat16)
    return (gate_pre, up_pre, hidden, outputs)


def direct_plan(tokens, routes, gates, cotangent, w_gate, w_up, w_down):
    rows_dev, width = tokens.shape
    picks = routes.shape[1]
    experts = lax.axis_size("expert")
    capacity = rows_dev * picks // experts
    gate_mat = w_gate[0]
    up_mat = w_up[0]
    down_mat = w_down[0]
    slots = slot_index(routes, experts, capacity)
    flat_rows = jnp.arange(rows_dev * picks, dtype=jnp.int32) // picks
    token_of = jnp.full((experts * capacity,), rows_dev, jnp.int32).at[slots].set(flat_rows)
    weight_of = jnp.zeros((experts * capacity,), jnp.float32).at[slots].set(gates.reshape(-1))
    token_pad = jnp.concatenate([tokens, jnp.zeros((1, width), tokens.dtype)], axis=0)
    send = token_pad[token_of].reshape(experts, capacity, width)

    def exchange(rows):
        return lax.all_to_all(
            rows.reshape(experts, capacity, width), "expert", split_axis=0, concat_axis=0, tiled=True
        )

    block = exchange(send)
    gate_pre, up_pre, hidden, outputs = expert_forward(block, gate_mat, up_mat, down_mat)
    back_items = exchange(outputs)
    inputs = block.reshape(-1, width)
    gathered = back_items.reshape(-1, width)[slots].reshape(rows_dev, picks, width)
    mixed = jnp.sum(gates[:, :, None] * gathered.astype(jnp.float32), axis=1).astype(jnp.bfloat16)
    cot_pad = jnp.concatenate([cotangent, jnp.zeros((1, width), cotangent.dtype)], axis=0)
    cot_send = (weight_of[:, None] * cot_pad[token_of].astype(jnp.float32)).astype(jnp.bfloat16)
    slot_cot = exchange(cot_send).reshape(-1, width)
    down_part = jnp.dot(hidden.T, slot_cot, preferred_element_type=jnp.float32)
    hidden_grad = jnp.dot(slot_cot, down_mat.T, preferred_element_type=jnp.float32)
    sigma = jax.nn.sigmoid(gate_pre)
    gate_grad = (hidden_grad * up_pre * sigma * (1.0 + gate_pre * (1.0 - sigma))).astype(
        jnp.bfloat16
    )
    up_grad = (hidden_grad * gate_pre * sigma).astype(jnp.bfloat16)
    slot_grads = (
        jnp.dot(gate_grad, gate_mat.T, preferred_element_type=jnp.float32)
        + jnp.dot(up_grad, up_mat.T, preferred_element_type=jnp.float32)
    ).astype(jnp.bfloat16)
    grads_back = exchange(slot_grads)
    gate_part = jnp.dot(inputs.T, gate_grad, preferred_element_type=jnp.float32)
    up_part = jnp.dot(inputs.T, up_grad, preferred_element_type=jnp.float32)
    grad_rows = grads_back.reshape(-1, width)[slots].reshape(rows_dev, picks, width)
    input_grad = jnp.sum(grad_rows.astype(jnp.float32), axis=1).astype(jnp.bfloat16)
    return (mixed, input_grad) + relay_sums(gate_part, up_part, down_part)


def relay_sums(*parts):
    relays = lax.axis_size("pipe")
    sums = []
    for part in parts:
        part = part.astype(BF)
        if relays == 2:
            other = lax.ppermute(part, "pipe", [(0, 1), (1, 0)])
            total = (part.astype(F32) + other.astype(F32)).astype(BF)
        else:
            total = lax.psum(part, "pipe")
        sums.append(total[None])
    return tuple(sums)


def chosen_rows(ids_ref, meta, picks, capacity):
    columns = meta.T
    routes, high, low = (columns[n * picks : (n + 1) * picks] for n in range(3))
    rows = meta.shape[0]
    member, weights = [], []
    for k in range(PLANE):
        hit = routes == ids_ref[k].astype(F32)
        member.append(jnp.sum(jnp.where(hit, 1.0, 0.0), axis=0, keepdims=True))
        weights.append(
            [jnp.sum(jnp.where(hit, part, 0.0), axis=0, keepdims=True) for part in (high, low)]
        )
    stacked = jnp.concatenate(member + [jnp.zeros((16 - PLANE, rows), F32)], axis=0)
    first = lax.broadcasted_iota(jnp.int32, (rows, rows), 0)
    second = lax.broadcasted_iota(jnp.int32, (rows, rows), 1)
    ahead = jnp.where(first < second, 1.0, 0.0).astype(BF)
    rank = jnp.dot(stacked.astype(BF), ahead, preferred_element_type=F32)
    slot = lax.broadcasted_iota(jnp.int32, (capacity, rows), 0).astype(F32)
    pick, pick_high, pick_low = [], [], []
    for k in range(PLANE):
        chosen = slot == jnp.where(member[k] > 0.5, rank[k : k + 1], -1.0)
        pick.append(jnp.where(chosen, 1.0, 0.0))
        pick_high.append(jnp.where(chosen, weights[k][0], 0.0))
        pick_low.append(jnp.where(chosen, weights[k][1], 0.0))
    return [jnp.concatenate(part, axis=0) for part in (pick, pick_high, pick_low)]


def put(out_refs, n, start, picked, capacity):
    for k, out_ref in enumerate(out_refs):
        out_ref[n, start : start + capacity] = picked[k * capacity : (k + 1) * capacity]


def picked_rows(matrices, block):
    return sum(jnp.dot(m, block, preferred_element_type=F32) for m in matrices).astype(BF)


def start_kernel(ids_ref, tokens_ref, routes_ref, gates_ref, cot_ref, block_ref, *refs, picks, capacity):
    table_ref, turned_ref, *out_refs = refs
    rows, width = tokens_ref.shape
    gates = gates_ref[...]
    high = gates.astype(BF).astype(F32)
    low = (gates - high).astype(BF).astype(F32)
    beside = [routes_ref[...].astype(F32), high, low, jnp.zeros((128 - 3 * picks, rows), F32)]
    meta = jnp.concatenate(beside, axis=0).T
    block_ref[:, :width] = tokens_ref[...]
    block_ref[:, width:] = meta.astype(BF)
    write_tables(ids_ref, meta, table_ref, turned_ref, 0, picks, capacity)
    put(out_refs, 0, 0, picked_rows([table_ref[0, 0]], tokens_ref[...]), capacity)
    rows = picked_rows([table_ref[0, 1], table_ref[0, 2]], cot_ref[...])
    put(out_refs, 0, capacity, rows, capacity)


def write_tables(ids_ref, meta, table_ref, turned_ref, n, picks, capacity):
    for m, table in enumerate(chosen_rows(ids_ref, meta, picks, capacity)):
        table_ref[n, m] = table.astype(BF)
        turned_ref[n, m] = table.T.astype(BF)


def table_shapes(count, capacity, rows):
    return [(count, 3, PLANE * capacity, rows), (count, 3, rows, PLANE * capacity)]


def start_rows(ids, tokens, routes, gates, cotangent, capacity):
    rows, width = tokens.shape
    picks = routes.shape[1]
    shapes = [(rows, width + 128)] + table_shapes(1, capacity, rows)
    shapes += [(1, 2 * capacity, width)] * PLANE
    block, table, turned, *out = pl.pallas_call(
        functools.partial(start_kernel, picks=picks, capacity=capacity),
        in_specs=[pl.BlockSpec(memory_space=pltpu.SMEM)]
        + [pl.BlockSpec(memory_space=pltpu.VMEM)] * 4,
        out_shape=[jax.ShapeDtypeStruct(s, BF) for s in shapes],
        compiler_params=pltpu.CompilerParams(vmem_limit_bytes=16 << 20),
        name="start_rows",
    )(ids, tokens, routes.T, gates.T, cotangent)
    return block, table, turned, out


def token_kernel(ids_ref, *refs, blocks, picks, capacity):
    meta_refs, row_refs, refs = refs[:blocks], refs[blocks : 2 * blocks], refs[2 * blocks :]
    table_ref, turned_ref, *out_refs = refs
    if blocks == 2:
        *out_refs, pass_ref = out_refs
        width = row_refs[0].shape[1]
        first = ids_ref[PLANE] == 1
        pass_ref[:, :width] = jnp.where(first, row_refs[0][...], row_refs[1][...])
        pass_ref[:, width:] = jnp.where(first, meta_refs[0][...], meta_refs[1][...])
    for n in range(blocks):
        meta = meta_refs[n][...].astype(F32)
        write_tables(ids_ref, meta, table_ref, turned_ref, n, picks, capacity)
        put(out_refs, n, 0, picked_rows([table_ref[n, 0]], row_refs[n][...]), capacity)


def token_rows(ids, blocks, picks, capacity):
    rows, wide = blocks[0].shape
    width, count = wide - 128, len(blocks)
    spec = [pl.BlockSpec((rows, 128), lambda i: (0, width // 128))] * count
    spec += [pl.BlockSpec((rows, width), lambda i: (0, 0))] * count
    shapes = table_shapes(count, capacity, rows) + [(count, capacity, width)] * PLANE
    if count == 2:
        shapes.append((rows, wide))
    table, turned, *out = pl.pallas_call(
        functools.partial(token_kernel, blocks=count, picks=picks, capacity=capacity),
        grid=(1,),
        in_specs=[pl.BlockSpec(memory_space=pltpu.SMEM)] + spec,
        out_specs=[pl.BlockSpec(s, lambda i, d=len(s): (0,) * d) for s in shapes],
        out_shape=[jax.ShapeDtypeStruct(s, BF) for s in shapes],
        compiler_params=pltpu.CompilerParams(vmem_limit_bytes=16 << 20),
        name="token_rows",
    )(ids, *blocks, *blocks)
    return table, turned, out


def cot_kernel(ids_ref, table_ref, *refs, blocks):
    row_refs, out_refs = refs[:blocks], refs[blocks:]
    if blocks == 2:
        *out_refs, pass_ref = out_refs
        pass_ref[...] = jnp.where(ids_ref[PLANE] == 1, row_refs[0][...], row_refs[1][...])
    for n in range(blocks):
        rows = picked_rows([table_ref[n, 1], table_ref[n, 2]], row_refs[n][...])
        put(out_refs, n, 0, rows, out_refs[0].shape[1])


def cot_rows(ids, table, blocks):
    rows, width = blocks[0].shape
    shapes = [(len(blocks), table.shape[2] // PLANE, width)] * PLANE
    if len(blocks) == 2:
        shapes.append((rows, width))
    return pl.pallas_call(
        functools.partial(cot_kernel, blocks=len(blocks)),
        in_specs=[pl.BlockSpec(memory_space=pltpu.SMEM)]
        + [pl.BlockSpec(memory_space=pltpu.VMEM)] * (1 + len(blocks)),
        out_shape=[jax.ShapeDtypeStruct(s, BF) for s in shapes],
        compiler_params=pltpu.CompilerParams(vmem_limit_bytes=16 << 20),
        name="cot_rows",
    )(ids, table, *blocks)


def expand_kernel(flags_ref, turned_ref, *refs, blocks, extras, parts, flagged):
    row_refs, extra_refs, out_refs = refs[:PLANE], refs[PLANE : PLANE + extras], refs[-blocks:]
    for n in range(blocks):
        rows = jnp.concatenate([ref[n] for ref in row_refs], axis=0)
        total = sum(jnp.dot(turned_ref[n, m], rows, preferred_element_type=F32) for m in parts)
        for ref in extra_refs:
            extra = ref[...].astype(F32)
            total += jnp.where(flags_ref[n] == 1, extra, 0.0) if flagged else extra
        out_refs[n][...] = total.astype(BF)


def expand(turned, rows, weighted, extras=(), flags=None):
    blocks, _, width = rows[0].shape
    rows_dev, slots = turned.shape[2:]
    work = 2 * blocks * rows_dev * slots * width * (2 if weighted else 1)
    moved = 2 * width * (blocks * (slots + rows_dev) + len(extras) * rows_dev)
    return pl.pallas_call(
        functools.partial(
            expand_kernel,
            blocks=blocks,
            extras=len(extras),
            parts=(1, 2) if weighted else (0,),
            flagged=flags is not None,
        ),
        in_specs=[pl.BlockSpec(memory_space=pltpu.SMEM)]
        + [pl.BlockSpec(memory_space=pltpu.VMEM)] * (1 + len(rows) + len(extras)),
        out_shape=[jax.ShapeDtypeStruct((rows_dev, width), BF)] * blocks,
        compiler_params=pltpu.CompilerParams(vmem_limit_bytes=16 << 20),
        cost_estimate=pl.CostEstimate(flops=work, bytes_accessed=moved, transcendentals=0),
        name="expand",
    )(jnp.zeros((2,), jnp.int32) if flags is None else flags, turned, *rows, *extras)


def nt_dot(a, b):
    return lax.dot_general(a, b, (((1,), (1,)), ((), ())), preferred_element_type=F32)


def forward_kernel(*refs, first):
    row_refs, (gate_ref, up_ref, down_ref), refs = refs[:PLANE], refs[PLANE : PLANE + 3], refs[PLANE + 3 :]
    gate_out, up_out, hidden_out, rows_out, *out_refs = refs
    count, capacity, width = out_refs[0].shape
    inputs = jnp.concatenate(
        [ref[n, :capacity] for ref in row_refs for n in range(count)], axis=0
    )
    rows_out[...] = inputs
    gate_pre = jnp.dot(inputs, gate_ref[...], preferred_element_type=F32)
    up_pre = jnp.dot(inputs, up_ref[...], preferred_element_type=F32)
    gate_out[...] = gate_pre
    up_out[...] = up_pre
    hidden = (gate_pre * jax.nn.sigmoid(gate_pre) * up_pre).astype(BF)
    hidden_out[...] = hidden.astype(F32).T.astype(BF)
    outputs = jnp.dot(hidden, down_ref[...], preferred_element_type=F32).astype(BF)
    for k, out_ref in enumerate(out_refs):
        for n in range(count):
            at = (k * count + n) * capacity
            out_ref[n] = outputs[at : at + capacity]


def forward(rows, capacity, gate_mat, up_mat, down_mat):
    count, _, width = rows[0].shape
    inner = gate_mat.shape[1]
    total = PLANE * count * capacity
    return pl.pallas_call(
        functools.partial(forward_kernel, first=capacity),
        out_shape=[
            jax.ShapeDtypeStruct((total, inner), F32),
            jax.ShapeDtypeStruct((total, inner), F32),
            jax.ShapeDtypeStruct((inner, total), BF),
            jax.ShapeDtypeStruct((total, width), BF),
        ]
        + [jax.ShapeDtypeStruct((count, capacity, width), BF)] * PLANE,
        compiler_params=pltpu.CompilerParams(vmem_limit_bytes=24 << 20),
        cost_estimate=pl.CostEstimate(
            flops=6 * total * width * inner,
            bytes_accessed=6 * width * inner + 6 * total * width + 10 * total * inner,
            transcendentals=total * inner,
        ),
        name="expert_forward",
    )(*rows, gate_mat, up_mat, down_mat)


def backward_kernel(*refs, skip):
    cot_refs, refs = refs[:PLANE], refs[PLANE:]
    gate_pre_ref, up_pre_ref, gate_ref, up_ref, down_ref, *refs = refs
    gate_out, up_out, rows_out, *out_refs = refs
    count, capacity, width = out_refs[0].shape
    cots = jnp.concatenate(
        [ref[n, skip : skip + capacity] for ref in cot_refs for n in range(count)], axis=0
    )
    rows_out[...] = cots
    hidden_grad = nt_dot(cots, down_ref[...])
    gate_pre, up_pre = gate_pre_ref[...], up_pre_ref[...]
    sigma = jax.nn.sigmoid(gate_pre)
    gate_grad = (hidden_grad * up_pre * sigma * (1.0 + gate_pre * (1.0 - sigma))).astype(BF)
    up_grad = (hidden_grad * gate_pre * sigma).astype(BF)
    gate_out[...] = gate_grad.astype(F32).T.astype(BF)
    up_out[...] = up_grad.astype(F32).T.astype(BF)
    grads = (nt_dot(gate_grad, gate_ref[...]) + nt_dot(up_grad, up_ref[...])).astype(BF)
    for k, out_ref in enumerate(out_refs):
        for n in range(count):
            at = (k * count + n) * capacity
            out_ref[n] = grads[at : at + capacity]


def backward(cots, skip, capacity, gate_pre, up_pre, gate_mat, up_mat, down_mat):
    count, _, width = cots[0].shape
    total, inner = gate_pre.shape
    return pl.pallas_call(
        functools.partial(backward_kernel, skip=skip),
        out_shape=[
            jax.ShapeDtypeStruct((inner, total), BF),
            jax.ShapeDtypeStruct((inner, total), BF),
            jax.ShapeDtypeStruct((total, width), BF),
        ]
        + [jax.ShapeDtypeStruct((count, capacity, width), BF)] * PLANE,
        compiler_params=pltpu.CompilerParams(vmem_limit_bytes=24 << 20),
        cost_estimate=pl.CostEstimate(
            flops=6 * total * width * inner,
            bytes_accessed=6 * width * inner + 6 * total * width + 12 * total * inner,
            transcendentals=total * inner,
        ),
        name="expert_backward",
    )(*cots, gate_pre, up_pre, gate_mat, up_mat, down_mat)


def partial_kernel(*refs):
    out_ref = refs[-1]
    chunks = (len(refs) - 1) // 5
    hidden, gate_grad, up_grad, inputs, cots = (
        refs[n * chunks : (n + 1) * chunks] for n in range(5)
    )
    for n, (left, right) in enumerate(((gate_grad, inputs), (up_grad, inputs), (hidden, cots))):
        total = sum(
            jnp.dot(a[...], b[...], preferred_element_type=F32) for a, b in zip(left, right)
        )
        out_ref[n] = total.astype(BF)


def partial_sums(hidden, gate_grad, up_grad, inputs, cots):
    inner, width = hidden[0].shape[0], inputs[0].shape[1]
    total = sum(a.shape[0] for a in inputs)
    tile = min(512, width)
    small = [*hidden, *gate_grad, *up_grad]
    large = [*inputs, *cots]
    return pl.pallas_call(
        partial_kernel,
        grid=(width // tile,),
        in_specs=[pl.BlockSpec(a.shape, lambda i: (0, 0)) for a in small]
        + [pl.BlockSpec((a.shape[0], tile), lambda i: (0, i)) for a in large],
        out_specs=pl.BlockSpec((3, inner, tile), lambda i: (0, 0, i)),
        out_shape=pltpu.HBM((3, inner, width), BF),
        compiler_params=pltpu.CompilerParams(vmem_limit_bytes=24 << 20),
        cost_estimate=pl.CostEstimate(
            flops=6 * total * inner * width,
            bytes_accessed=6 * total * inner + 4 * total * width + 6 * inner * width,
            transcendentals=0,
        ),
        name="partial_sums",
    )(*small, *large)


def turn_kernel(*refs):
    *sum_refs, gate_ref, up_ref, down_ref = refs
    for n, out_ref in enumerate((gate_ref, up_ref, down_ref)):
        total = sum(ref[n].astype(F32) for ref in sum_refs)
        out_ref[0] = (total if n == 2 else total.T).astype(BF)


def weight_outputs(*sums):
    _, inner, width = sums[0].shape
    tile = min(512, width)
    return pl.pallas_call(
        turn_kernel,
        grid=(width // tile,),
        in_specs=[pl.BlockSpec((3, inner, tile), lambda i: (0, 0, i))] * len(sums),
        out_specs=[
            pl.BlockSpec((1, tile, inner), lambda i: (0, i, 0)),
            pl.BlockSpec((1, tile, inner), lambda i: (0, i, 0)),
            pl.BlockSpec((1, inner, tile), lambda i: (0, 0, i)),
        ],
        out_shape=[
            jax.ShapeDtypeStruct((1, width, inner), BF),
            jax.ShapeDtypeStruct((1, width, inner), BF),
            jax.ShapeDtypeStruct((1, inner, width), BF),
        ],
        compiler_params=pltpu.CompilerParams(vmem_limit_bytes=16 << 20),
        cost_estimate=pl.CostEstimate(
            flops=6 * inner * width,
            bytes_accessed=6 * inner * width * (1 + len(sums)),
            transcendentals=0,
        ),
        name="weight_outputs",
    )(*sums)


def plane_plan(tokens, routes, gates, cotangent, w_gate, w_up, w_down):
    rows_dev, width = tokens.shape
    picks = routes.shape[1]
    experts = lax.axis_size("expert")
    capacity = rows_dev * picks // experts
    mats = (w_gate[0], w_up[0], w_down[0])
    here = lax.axis_index("expert")
    level, place = here // PLANE, here % PLANE
    odd = level % 2
    ids = jnp.stack([level * PLANE + (place ^ k) for k in range(PLANE)] + [odd])

    def permute(value, step):
        pairs = [(i, step(i // PLANE) % LEVELS * PLANE + i % PLANE) for i in range(experts)]
        return lax.ppermute(value, "expert", pairs)

    def from_above(value):
        return permute(value, lambda n: n - 1)

    def from_below(value):
        return permute(value, lambda n: n + 1)

    def swap(value):
        return permute(value, lambda n: n ^ 1)

    stages = []

    def across(rows, *deps):
        sent = tuple(rows[1:])
        if stages or deps:
            sent, *_ = lax.optimization_barrier((sent, *stages[-1:], *deps))
        moved = {
            k: lax.ppermute(sent[k - 1], "expert", [(i, i ^ k) for i in range(experts)])
            for k in (3, 1, 2)
        }
        stages.append(tuple(moved[k] for k in range(1, PLANE)))
        return [rows[0], *stages[-1]]

    block, table_a, turned_a, rows_a = start_rows(ids, tokens, routes, gates, cotangent, capacity)
    rows_a = across(rows_a)
    above, below = from_above(block), from_below(block)
    table_b, turned_b, (*rows_b, far) = token_rows(ids, [above, below], picks, capacity)
    far = swap(far)
    rows_b = across(rows_b)
    later, far = lax.optimization_barrier((cotangent, far))
    cot_above, cot_below = from_above(later), from_below(later)
    table_c, turned_c, rows_c = token_rows(ids, [far], picks, capacity)
    rows_c = across(rows_c)
    *cots_b, cot_far = cot_rows(ids, table_b, [cot_above, cot_below])
    cot_far = swap(cot_far)
    cots_b = across(cots_b)

    saved = [forward(rows, capacity, *mats) for rows in (rows_a, rows_b, rows_c)]
    outs = [s[4:] for s in saved]

    def back(cots, skip, forth):
        return backward(cots, skip, capacity, forth[0], forth[1], *mats)

    back_a = back(rows_a, capacity, saved[0])
    cots_c = across(cot_rows(ids, table_c, [cot_far]), saved, back_a)
    back_b = back(cots_b, 0, saved[1])
    mixed_c = across(outs[2], back_b)
    back_c = back(cots_c, 0, saved[2])
    backs = (back_a, back_b, back_c)
    partial = partial_sums(
        [s[2] for s in saved],
        [b[0] for b in backs],
        [b[1] for b in backs],
        [s[3] for s in saved],
        [b[2] for b in backs],
    )
    grads_c = across(back_c[3:], partial)
    passed = jnp.stack([odd, 1 - odd])

    def send_near(rows, weighted, far, *deps):
        near = expand(turned_b, rows, weighted, [far], passed)
        near, *_ = lax.optimization_barrier((near, *deps))
        return from_below(near[0]), from_above(near[1])

    mixed_far = swap(*expand(turned_c, mixed_c, True))
    sent, _ = lax.optimization_barrier((partial, mixed_c))
    other = lax.ppermute(sent, "pipe", [(0, 1), (1, 0)])
    mixed_b = across(outs[1])
    grads_far = swap(*expand(turned_c, grads_c, False))
    weight_grads = weight_outputs(partial, other)
    grads_b = across(back_b[3:], mixed_far, grads_far, weight_grads)
    mixed_near = send_near(mixed_b, True, mixed_far, grads_far)
    mixed_a = across(outs[0])
    grads_near = send_near(grads_b, False, grads_far, mixed_near)
    grads_a = across(back_a[3:], mixed_near)
    mixed = expand(turned_a, mixed_a, True, mixed_near)
    input_grad = expand(turned_a, grads_a, False, grads_near)
    return (*mixed, *input_grad, *weight_grads)


def on_device(tokens, routes, *rest):
    experts, picks = lax.axis_size("expert"), routes.shape[1]
    if experts == LEVELS * PLANE and lax.axis_size("pipe") == 2 and experts <= 2 * picks:
        return plane_plan(tokens, routes, *rest)
    return direct_plan(tokens, routes, *rest)


def solution(mesh):
    rows, stack = P(("pipe", "expert"), None), P("expert", None, None)
    return jax.shard_map(
        on_device,
        mesh=mesh,
        in_specs=(rows, rows, rows, rows, stack, stack, stack),
        out_specs=(rows, rows, stack, stack, stack),
        check_vma=False,
    )
```

```python
import functools

import jax
import jax.numpy as jnp
from jax import lax
from jax.experimental import pallas as pl
from jax.experimental.pallas import tpu as pltpu
from jax.sharding import PartitionSpec as P

PLANE = 4
LEVELS = 4
BF = jnp.bfloat16
F32 = jnp.float32


def slot_index(block_routes, expert_count, capacity):
    flat = block_routes.reshape(-1)
    onehot = (flat[:, None] == jnp.arange(expert_count, dtype=jnp.int32)[None, :]).astype(jnp.int32)
    before = jnp.cumsum(onehot, axis=0) - onehot
    ranks = jnp.sum(before * onehot, axis=1)
    return flat * capacity + ranks


def expert_forward(block, gate_mat, up_mat, down_mat):
    inputs = block.reshape(-1, block.shape[2])
    gate_pre = jnp.dot(inputs, gate_mat, preferred_element_type=jnp.float32)
    up_pre = jnp.dot(inputs, up_mat, preferred_element_type=jnp.float32)
    sigma = jax.nn.sigmoid(gate_pre)
    hidden = (gate_pre * sigma * up_pre).astype(jnp.bfloat16)
    outputs = jnp.dot(hidden, down_mat, preferred_element_type=jnp.float32).astype(jnp.bfloat16)
    return (gate_pre, up_pre, hidden, outputs)


def direct_plan(tokens, routes, gates, cotangent, w_gate, w_up, w_down):
    rows_dev, width = tokens.shape
    picks = routes.shape[1]
    experts = lax.axis_size("expert")
    capacity = rows_dev * picks // experts
    gate_mat = w_gate[0]
    up_mat = w_up[0]
    down_mat = w_down[0]
    slots = slot_index(routes, experts, capacity)
    flat_rows = jnp.arange(rows_dev * picks, dtype=jnp.int32) // picks
    token_of = jnp.full((experts * capacity,), rows_dev, jnp.int32).at[slots].set(flat_rows)
    weight_of = jnp.zeros((experts * capacity,), jnp.float32).at[slots].set(gates.reshape(-1))
    token_pad = jnp.concatenate([tokens, jnp.zeros((1, width), tokens.dtype)], axis=0)
    send = token_pad[token_of].reshape(experts, capacity, width)

    def exchange(rows):
        return lax.all_to_all(
            rows.reshape(experts, capacity, width), "expert", split_axis=0, concat_axis=0, tiled=True
        )

    block = exchange(send)
    gate_pre, up_pre, hidden, outputs = expert_forward(block, gate_mat, up_mat, down_mat)
    back_items = exchange(outputs)
    inputs = block.reshape(-1, width)
    gathered = back_items.reshape(-1, width)[slots].reshape(rows_dev, picks, width)
    mixed = jnp.sum(gates[:, :, None] * gathered.astype(jnp.float32), axis=1).astype(jnp.bfloat16)
    cot_pad = jnp.concatenate([cotangent, jnp.zeros((1, width), cotangent.dtype)], axis=0)
    cot_send = (weight_of[:, None] * cot_pad[token_of].astype(jnp.float32)).astype(jnp.bfloat16)
    slot_cot = exchange(cot_send).reshape(-1, width)
    down_part = jnp.dot(hidden.T, slot_cot, preferred_element_type=jnp.float32)
    hidden_grad = jnp.dot(slot_cot, down_mat.T, preferred_element_type=jnp.float32)
    sigma = jax.nn.sigmoid(gate_pre)
    gate_grad = (hidden_grad * up_pre * sigma * (1.0 + gate_pre * (1.0 - sigma))).astype(
        jnp.bfloat16
    )
    up_grad = (hidden_grad * gate_pre * sigma).astype(jnp.bfloat16)
    slot_grads = (
        jnp.dot(gate_grad, gate_mat.T, preferred_element_type=jnp.float32)
        + jnp.dot(up_grad, up_mat.T, preferred_element_type=jnp.float32)
    ).astype(jnp.bfloat16)
    grads_back = exchange(slot_grads)
    gate_part = jnp.dot(inputs.T, gate_grad, preferred_element_type=jnp.float32)
    up_part = jnp.dot(inputs.T, up_grad, preferred_element_type=jnp.float32)
    grad_rows = grads_back.reshape(-1, width)[slots].reshape(rows_dev, picks, width)
    input_grad = jnp.sum(grad_rows.astype(jnp.float32), axis=1).astype(jnp.bfloat16)
    return (mixed, input_grad) + relay_sums(gate_part, up_part, down_part)


def relay_sums(*parts):
    relays = lax.axis_size("pipe")
    sums = []
    for part in parts:
        part = part.astype(BF)
        if relays == 2:
            other = lax.ppermute(part, "pipe", [(0, 1), (1, 0)])
            total = (part.astype(F32) + other.astype(F32)).astype(BF)
        else:
            total = lax.psum(part, "pipe")
        sums.append(total[None])
    return tuple(sums)


def chosen_rows(ids_ref, meta, picks, capacity):
    columns = meta.T
    routes, high, low = (columns[n * picks : (n + 1) * picks] for n in range(3))
    rows = meta.shape[0]
    member, weights = [], []
    for k in range(PLANE):
        hit = routes == ids_ref[k].astype(F32)
        member.append(jnp.sum(jnp.where(hit, 1.0, 0.0), axis=0, keepdims=True))
        weights.append(
            [jnp.sum(jnp.where(hit, part, 0.0), axis=0, keepdims=True) for part in (high, low)]
        )
    stacked = jnp.concatenate(member + [jnp.zeros((16 - PLANE, rows), F32)], axis=0)
    first = lax.broadcasted_iota(jnp.int32, (rows, rows), 0)
    second = lax.broadcasted_iota(jnp.int32, (rows, rows), 1)
    ahead = jnp.where(first < second, 1.0, 0.0).astype(BF)
    rank = jnp.dot(stacked.astype(BF), ahead, preferred_element_type=F32)
    slot = lax.broadcasted_iota(jnp.int32, (capacity, rows), 0).astype(F32)
    pick, pick_high, pick_low = [], [], []
    for k in range(PLANE):
        chosen = slot == jnp.where(member[k] > 0.5, rank[k : k + 1], -1.0)
        pick.append(jnp.where(chosen, 1.0, 0.0))
        pick_high.append(jnp.where(chosen, weights[k][0], 0.0))
        pick_low.append(jnp.where(chosen, weights[k][1], 0.0))
    return [jnp.concatenate(part, axis=0) for part in (pick, pick_high, pick_low)]


def put(out_refs, n, start, picked, capacity):
    for k, out_ref in enumerate(out_refs):
        out_ref[n, start : start + capacity] = picked[k * capacity : (k + 1) * capacity]


def picked_rows(matrices, block):
    return sum(jnp.dot(m, block, preferred_element_type=F32) for m in matrices).astype(BF)


def start_kernel(ids_ref, *refs, picks, capacity):
    sources, block_ref, table_ref, turned_ref = refs[:4], *refs[4:7]
    out_refs, held, arrived = refs[7 : 7 + PLANE], refs[7 + PLANE : -1], refs[-1]
    copies = [
        pltpu.make_async_copy(source, target, arrived.at[n])
        for n, (source, target) in enumerate(zip(sources, held))
    ]
    for copy in copies:
        copy.start()
    for copy in copies:
        copy.wait()
    tokens_ref, routes_ref, gates_ref, cot_ref = held
    rows, width = tokens_ref.shape
    gates = gates_ref[...]
    high = gates.astype(BF).astype(F32)
    low = (gates - high).astype(BF).astype(F32)
    beside = [routes_ref[...].astype(F32), high, low, jnp.zeros((128 - 3 * picks, rows), F32)]
    meta = jnp.concatenate(beside, axis=0).T
    block_ref[:, :width] = tokens_ref[...]
    block_ref[:, width:] = meta.astype(BF)
    write_tables(ids_ref, meta, table_ref, turned_ref, 0, picks, capacity)
    put(out_refs, 0, 0, picked_rows([table_ref[0, 0]], tokens_ref[...]), capacity)
    rows = picked_rows([table_ref[0, 1], table_ref[0, 2]], cot_ref[...])
    put(out_refs, 0, capacity, rows, capacity)


def write_tables(ids_ref, meta, table_ref, turned_ref, n, picks, capacity):
    for m, table in enumerate(chosen_rows(ids_ref, meta, picks, capacity)):
        table_ref[n, m] = table.astype(BF)
        turned_ref[n, m] = table.T.astype(BF)


def table_shapes(count, capacity, rows):
    return [(count, 3, PLANE * capacity, rows), (count, 3, rows, PLANE * capacity)]


def start_rows(ids, tokens, routes, gates, cotangent, capacity):
    rows, width = tokens.shape
    picks = routes.shape[1]
    shapes = [(rows, width + 128)] + table_shapes(1, capacity, rows)
    shapes += [(1, 2 * capacity, width)] * PLANE
    block, table, turned, *out = pl.pallas_call(
        functools.partial(start_kernel, picks=picks, capacity=capacity),
        in_specs=[pl.BlockSpec(memory_space=pltpu.SMEM)]
        + [pl.BlockSpec(memory_space=pltpu.HBM)] * 4,
        out_shape=[jax.ShapeDtypeStruct(s, BF) for s in shapes],
        scratch_shapes=[
            pltpu.VMEM((rows, width), BF),
            pltpu.VMEM((picks, rows), routes.dtype),
            pltpu.VMEM((picks, rows), gates.dtype),
            pltpu.VMEM((rows, width), BF),
            pltpu.SemaphoreType.DMA((4,)),
        ],
        compiler_params=pltpu.CompilerParams(vmem_limit_bytes=16 << 20),
        name="start_rows",
    )(ids, *(pltpu.with_memory_space_constraint(v, pltpu.HBM) for v in (tokens, routes.T, gates.T, cotangent)))
    return block, table, turned, out


def token_kernel(ids_ref, *refs, blocks, picks, capacity):
    meta_refs, row_refs, refs = refs[:blocks], refs[blocks : 2 * blocks], refs[2 * blocks :]
    table_ref, turned_ref, *out_refs = refs
    if blocks == 2:
        *out_refs, pass_ref = out_refs
        width = row_refs[0].shape[1]
        first = ids_ref[PLANE] == 1
        pass_ref[:, :width] = jnp.where(first, row_refs[0][...], row_refs[1][...])
        pass_ref[:, width:] = jnp.where(first, meta_refs[0][...], meta_refs[1][...])
    for n in range(blocks):
        meta = meta_refs[n][...].astype(F32)
        write_tables(ids_ref, meta, table_ref, turned_ref, n, picks, capacity)
        put(out_refs, n, 0, picked_rows([table_ref[n, 0]], row_refs[n][...]), capacity)


def token_rows(ids, blocks, picks, capacity):
    rows, wide = blocks[0].shape
    width, count = wide - 128, len(blocks)
    spec = [pl.BlockSpec((rows, 128), lambda i: (0, width // 128))] * count
    spec += [pl.BlockSpec((rows, width), lambda i: (0, 0))] * count
    shapes = table_shapes(count, capacity, rows) + [(count, capacity, width)] * PLANE
    if count == 2:
        shapes.append((rows, wide))
    table, turned, *out = pl.pallas_call(
        functools.partial(token_kernel, blocks=count, picks=picks, capacity=capacity),
        grid=(1,),
        in_specs=[pl.BlockSpec(memory_space=pltpu.SMEM)] + spec,
        out_specs=[pl.BlockSpec(s, lambda i, d=len(s): (0,) * d) for s in shapes],
        out_shape=[jax.ShapeDtypeStruct(s, BF) for s in shapes],
        compiler_params=pltpu.CompilerParams(vmem_limit_bytes=16 << 20),
        name="token_rows",
    )(ids, *blocks, *blocks)
    return table, turned, out


def cot_kernel(ids_ref, table_ref, *refs, blocks):
    row_refs, out_refs = refs[:blocks], refs[blocks:]
    if blocks == 2:
        *out_refs, pass_ref = out_refs
        pass_ref[...] = jnp.where(ids_ref[PLANE] == 1, row_refs[0][...], row_refs[1][...])
    for n in range(blocks):
        rows = picked_rows([table_ref[n, 1], table_ref[n, 2]], row_refs[n][...])
        put(out_refs, n, 0, rows, out_refs[0].shape[1])


def cot_rows(ids, table, blocks):
    rows, width = blocks[0].shape
    shapes = [(len(blocks), table.shape[2] // PLANE, width)] * PLANE
    if len(blocks) == 2:
        shapes.append((rows, width))
    return pl.pallas_call(
        functools.partial(cot_kernel, blocks=len(blocks)),
        in_specs=[pl.BlockSpec(memory_space=pltpu.SMEM)]
        + [pl.BlockSpec(memory_space=pltpu.VMEM)] * (1 + len(blocks)),
        out_shape=[jax.ShapeDtypeStruct(s, BF) for s in shapes],
        compiler_params=pltpu.CompilerParams(vmem_limit_bytes=16 << 20),
        name="cot_rows",
    )(ids, table, *blocks)


def expand_kernel(flags_ref, turned_ref, *refs, blocks, extras, parts, flagged):
    row_refs, extra_refs, out_refs = refs[:PLANE], refs[PLANE : PLANE + extras], refs[-blocks:]
    for n in range(blocks):
        rows = jnp.concatenate([ref[n] for ref in row_refs], axis=0)
        total = sum(jnp.dot(turned_ref[n, m], rows, preferred_element_type=F32) for m in parts)
        for ref in extra_refs:
            extra = ref[...].astype(F32)
            total += jnp.where(flags_ref[n] == 1, extra, 0.0) if flagged else extra
        out_refs[n][...] = total.astype(BF)


def expand(turned, rows, weighted, extras=(), flags=None):
    blocks, _, width = rows[0].shape
    rows_dev, slots = turned.shape[2:]
    work = 2 * blocks * rows_dev * slots * width * (2 if weighted else 1)
    moved = 2 * width * (blocks * (slots + rows_dev) + len(extras) * rows_dev)
    return pl.pallas_call(
        functools.partial(
            expand_kernel,
            blocks=blocks,
            extras=len(extras),
            parts=(1, 2) if weighted else (0,),
            flagged=flags is not None,
        ),
        in_specs=[pl.BlockSpec(memory_space=pltpu.SMEM)]
        + [pl.BlockSpec(memory_space=pltpu.VMEM)] * (1 + len(rows) + len(extras)),
        out_shape=[jax.ShapeDtypeStruct((rows_dev, width), BF)] * blocks,
        compiler_params=pltpu.CompilerParams(vmem_limit_bytes=16 << 20),
        cost_estimate=pl.CostEstimate(flops=work, bytes_accessed=moved, transcendentals=0),
        name="expand",
    )(jnp.zeros((2,), jnp.int32) if flags is None else flags, turned, *rows, *extras)


def nt_dot(a, b):
    return lax.dot_general(a, b, (((1,), (1,)), ((), ())), preferred_element_type=F32)


def forward_kernel(*refs, first):
    row_refs, (gate_ref, up_ref, down_ref), refs = refs[:PLANE], refs[PLANE : PLANE + 3], refs[PLANE + 3 :]
    gate_out, up_out, hidden_out, rows_out, *out_refs = refs
    count, capacity, width = out_refs[0].shape
    inputs = jnp.concatenate(
        [ref[n, :capacity] for ref in row_refs for n in range(count)], axis=0
    )
    rows_out[...] = inputs
    gate_pre = jnp.dot(inputs, gate_ref[...], preferred_element_type=F32)
    up_pre = jnp.dot(inputs, up_ref[...], preferred_element_type=F32)
    gate_out[...] = gate_pre
    up_out[...] = up_pre
    hidden = (gate_pre * jax.nn.sigmoid(gate_pre) * up_pre).astype(BF)
    hidden_out[...] = hidden.astype(F32).T.astype(BF)
    outputs = jnp.dot(hidden, down_ref[...], preferred_element_type=F32).astype(BF)
    for k, out_ref in enumerate(out_refs):
        for n in range(count):
            at = (k * count + n) * capacity
            out_ref[n] = outputs[at : at + capacity]


def forward(rows, capacity, gate_mat, up_mat, down_mat):
    count, _, width = rows[0].shape
    inner = gate_mat.shape[1]
    total = PLANE * count * capacity
    return pl.pallas_call(
        functools.partial(forward_kernel, first=capacity),
        out_shape=[
            jax.ShapeDtypeStruct((total, inner), F32),
            jax.ShapeDtypeStruct((total, inner), F32),
            jax.ShapeDtypeStruct((inner, total), BF),
            jax.ShapeDtypeStruct((total, width), BF),
        ]
        + [jax.ShapeDtypeStruct((count, capacity, width), BF)] * PLANE,
        compiler_params=pltpu.CompilerParams(vmem_limit_bytes=24 << 20),
        cost_estimate=pl.CostEstimate(
            flops=6 * total * width * inner,
            bytes_accessed=6 * width * inner + 6 * total * width + 10 * total * inner,
            transcendentals=total * inner,
        ),
        name="expert_forward",
    )(*rows, gate_mat, up_mat, down_mat)


def backward_kernel(*refs, skip):
    cot_refs, refs = refs[:PLANE], refs[PLANE:]
    gate_pre_ref, up_pre_ref, gate_ref, up_ref, down_ref, *refs = refs
    gate_out, up_out, rows_out, *out_refs = refs
    count, capacity, width = out_refs[0].shape
    cots = jnp.concatenate(
        [ref[n, skip : skip + capacity] for ref in cot_refs for n in range(count)], axis=0
    )
    rows_out[...] = cots
    hidden_grad = nt_dot(cots, down_ref[...])
    gate_pre, up_pre = gate_pre_ref[...], up_pre_ref[...]
    sigma = jax.nn.sigmoid(gate_pre)
    gate_grad = (hidden_grad * up_pre * sigma * (1.0 + gate_pre * (1.0 - sigma))).astype(BF)
    up_grad = (hidden_grad * gate_pre * sigma).astype(BF)
    gate_out[...] = gate_grad.astype(F32).T.astype(BF)
    up_out[...] = up_grad.astype(F32).T.astype(BF)
    grads = (nt_dot(gate_grad, gate_ref[...]) + nt_dot(up_grad, up_ref[...])).astype(BF)
    for k, out_ref in enumerate(out_refs):
        for n in range(count):
            at = (k * count + n) * capacity
            out_ref[n] = grads[at : at + capacity]


def backward(cots, skip, capacity, gate_pre, up_pre, gate_mat, up_mat, down_mat):
    count, _, width = cots[0].shape
    total, inner = gate_pre.shape
    return pl.pallas_call(
        functools.partial(backward_kernel, skip=skip),
        out_shape=[
            jax.ShapeDtypeStruct((inner, total), BF),
            jax.ShapeDtypeStruct((inner, total), BF),
            jax.ShapeDtypeStruct((total, width), BF),
        ]
        + [jax.ShapeDtypeStruct((count, capacity, width), BF)] * PLANE,
        compiler_params=pltpu.CompilerParams(vmem_limit_bytes=24 << 20),
        cost_estimate=pl.CostEstimate(
            flops=6 * total * width * inner,
            bytes_accessed=6 * width * inner + 6 * total * width + 12 * total * inner,
            transcendentals=total * inner,
        ),
        name="expert_backward",
    )(*cots, gate_pre, up_pre, gate_mat, up_mat, down_mat)


def partial_kernel(*refs):
    out_ref = refs[-1]
    chunks = (len(refs) - 1) // 5
    hidden, gate_grad, up_grad, inputs, cots = (
        refs[n * chunks : (n + 1) * chunks] for n in range(5)
    )
    for n, (left, right) in enumerate(((gate_grad, inputs), (up_grad, inputs), (hidden, cots))):
        total = sum(
            jnp.dot(a[...], b[...], preferred_element_type=F32) for a, b in zip(left, right)
        )
        out_ref[n] = total.astype(BF)


def partial_sums(hidden, gate_grad, up_grad, inputs, cots):
    inner, width = hidden[0].shape[0], inputs[0].shape[1]
    total = sum(a.shape[0] for a in inputs)
    tile = min(512, width)
    small = [*hidden, *gate_grad, *up_grad]
    large = [*inputs, *cots]
    return pl.pallas_call(
        partial_kernel,
        grid=(width // tile,),
        in_specs=[pl.BlockSpec(a.shape, lambda i: (0, 0)) for a in small]
        + [pl.BlockSpec((a.shape[0], tile), lambda i: (0, i)) for a in large],
        out_specs=pl.BlockSpec((3, inner, tile), lambda i: (0, 0, i)),
        out_shape=pltpu.HBM((3, inner, width), BF),
        compiler_params=pltpu.CompilerParams(vmem_limit_bytes=24 << 20),
        cost_estimate=pl.CostEstimate(
            flops=6 * total * inner * width,
            bytes_accessed=6 * total * inner + 4 * total * width + 6 * inner * width,
            transcendentals=0,
        ),
        name="partial_sums",
    )(*small, *large)


def turn_kernel(*refs):
    *sum_refs, gate_ref, up_ref, down_ref = refs
    for n, out_ref in enumerate((gate_ref, up_ref, down_ref)):
        total = sum(ref[n].astype(F32) for ref in sum_refs)
        out_ref[0] = (total if n == 2 else total.T).astype(BF)


def weight_outputs(*sums):
    _, inner, width = sums[0].shape
    tile = min(512, width)
    return pl.pallas_call(
        turn_kernel,
        grid=(width // tile,),
        in_specs=[pl.BlockSpec((3, inner, tile), lambda i: (0, 0, i))] * len(sums),
        out_specs=[
            pl.BlockSpec((1, tile, inner), lambda i: (0, i, 0)),
            pl.BlockSpec((1, tile, inner), lambda i: (0, i, 0)),
            pl.BlockSpec((1, inner, tile), lambda i: (0, 0, i)),
        ],
        out_shape=[
            jax.ShapeDtypeStruct((1, width, inner), BF),
            jax.ShapeDtypeStruct((1, width, inner), BF),
            jax.ShapeDtypeStruct((1, inner, width), BF),
        ],
        compiler_params=pltpu.CompilerParams(vmem_limit_bytes=16 << 20),
        cost_estimate=pl.CostEstimate(
            flops=6 * inner * width,
            bytes_accessed=6 * inner * width * (1 + len(sums)),
            transcendentals=0,
        ),
        name="weight_outputs",
    )(*sums)


def plane_plan(tokens, routes, gates, cotangent, w_gate, w_up, w_down):
    rows_dev, width = tokens.shape
    picks = routes.shape[1]
    experts = lax.axis_size("expert")
    capacity = rows_dev * picks // experts
    mats = (w_gate[0], w_up[0], w_down[0])
    here = lax.axis_index("expert")
    level, place = here // PLANE, here % PLANE
    odd = level % 2
    ids = jnp.stack([level * PLANE + (place ^ k) for k in range(PLANE)] + [odd])

    def permute(value, step):
        pairs = [(i, step(i // PLANE) % LEVELS * PLANE + i % PLANE) for i in range(experts)]
        return lax.ppermute(value, "expert", pairs)

    def from_above(value):
        return permute(value, lambda n: n - 1)

    def from_below(value):
        return permute(value, lambda n: n + 1)

    def swap(value):
        return permute(value, lambda n: n ^ 1)

    stages = []

    def across(rows, *deps):
        sent = tuple(rows[1:])
        if stages or deps:
            sent, *_ = lax.optimization_barrier((sent, *stages[-1:], *deps))
        moved = {
            k: lax.ppermute(sent[k - 1], "expert", [(i, i ^ k) for i in range(experts)])
            for k in (3, 1, 2)
        }
        stages.append(tuple(moved[k] for k in range(1, PLANE)))
        return [rows[0], *stages[-1]]

    block, table_a, turned_a, rows_a = start_rows(ids, tokens, routes, gates, cotangent, capacity)
    rows_a = across(rows_a)
    above, below = from_above(block), from_below(block)
    table_b, turned_b, (*rows_b, far) = token_rows(ids, [above, below], picks, capacity)
    far = swap(far)
    rows_b = across(rows_b)
    later, far = lax.optimization_barrier((cotangent, far))
    cot_above, cot_below = from_above(later), from_below(later)
    table_c, turned_c, rows_c = token_rows(ids, [far], picks, capacity)
    rows_c = across(rows_c)
    *cots_b, cot_far = cot_rows(ids, table_b, [cot_above, cot_below])
    cot_far = swap(cot_far)
    cots_b = across(cots_b)

    saved = [forward(rows, capacity, *mats) for rows in (rows_a, rows_b, rows_c)]
    outs = [s[4:] for s in saved]

    def back(cots, skip, forth):
        return backward(cots, skip, capacity, forth[0], forth[1], *mats)

    back_a = back(rows_a, capacity, saved[0])
    cots_c = across(cot_rows(ids, table_c, [cot_far]), saved, back_a)
    back_b = back(cots_b, 0, saved[1])
    mixed_c = across(outs[2], back_b)
    back_c = back(cots_c, 0, saved[2])
    backs = (back_a, back_b, back_c)
    partial = partial_sums(
        [s[2] for s in saved],
        [b[0] for b in backs],
        [b[1] for b in backs],
        [s[3] for s in saved],
        [b[2] for b in backs],
    )
    grads_c = across(back_c[3:], partial)
    passed = jnp.stack([odd, 1 - odd])

    def send_near(rows, weighted, far, *deps):
        near = expand(turned_b, rows, weighted, [far], passed)
        near, *_ = lax.optimization_barrier((near, *deps))
        return from_below(near[0]), from_above(near[1])

    mixed_far = swap(*expand(turned_c, mixed_c, True))
    sent, _ = lax.optimization_barrier((partial, mixed_c))
    other = lax.ppermute(sent, "pipe", [(0, 1), (1, 0)])
    mixed_b = across(outs[1])
    grads_far = swap(*expand(turned_c, grads_c, False))
    weight_grads = weight_outputs(partial, other)
    grads_b = across(back_b[3:], mixed_far, grads_far, weight_grads)
    mixed_near = send_near(mixed_b, True, mixed_far, grads_far)
    mixed_a = across(outs[0])
    grads_near = send_near(grads_b, False, grads_far, mixed_near)
    grads_a = across(back_a[3:], mixed_near)
    mixed = expand(turned_a, mixed_a, True, mixed_near)
    input_grad = expand(turned_a, grads_a, False, grads_near)
    return (*mixed, *input_grad, *weight_grads)


def on_device(tokens, routes, *rest):
    experts, picks = lax.axis_size("expert"), routes.shape[1]
    if experts == LEVELS * PLANE and lax.axis_size("pipe") == 2 and experts <= 2 * picks:
        return plane_plan(tokens, routes, *rest)
    return direct_plan(tokens, routes, *rest)


def solution(mesh):
    rows, stack = P(("pipe", "expert"), None), P("expert", None, None)
    return jax.shard_map(
        on_device,
        mesh=mesh,
        in_specs=(rows, rows, rows, rows, stack, stack, stack),
        out_specs=(rows, rows, stack, stack, stack),
        check_vma=False,
    )
```

```python
import functools

import jax
import jax.numpy as jnp
from jax import lax
from jax.experimental import pallas as pl
from jax.experimental.pallas import tpu as pltpu
from jax.sharding import PartitionSpec as P

PLANE = 4
LEVELS = 4
BF = jnp.bfloat16
F32 = jnp.float32


def slot_index(block_routes, expert_count, capacity):
    flat = block_routes.reshape(-1)
    onehot = (flat[:, None] == jnp.arange(expert_count, dtype=jnp.int32)[None, :]).astype(jnp.int32)
    before = jnp.cumsum(onehot, axis=0) - onehot
    ranks = jnp.sum(before * onehot, axis=1)
    return flat * capacity + ranks


def expert_forward(block, gate_mat, up_mat, down_mat):
    inputs = block.reshape(-1, block.shape[2])
    gate_pre = jnp.dot(inputs, gate_mat, preferred_element_type=jnp.float32)
    up_pre = jnp.dot(inputs, up_mat, preferred_element_type=jnp.float32)
    sigma = jax.nn.sigmoid(gate_pre)
    hidden = (gate_pre * sigma * up_pre).astype(jnp.bfloat16)
    outputs = jnp.dot(hidden, down_mat, preferred_element_type=jnp.float32).astype(jnp.bfloat16)
    return (gate_pre, up_pre, hidden, outputs)


def direct_plan(tokens, routes, gates, cotangent, w_gate, w_up, w_down):
    rows_dev, width = tokens.shape
    picks = routes.shape[1]
    experts = lax.axis_size("expert")
    capacity = rows_dev * picks // experts
    gate_mat = w_gate[0]
    up_mat = w_up[0]
    down_mat = w_down[0]
    slots = slot_index(routes, experts, capacity)
    flat_rows = jnp.arange(rows_dev * picks, dtype=jnp.int32) // picks
    token_of = jnp.full((experts * capacity,), rows_dev, jnp.int32).at[slots].set(flat_rows)
    weight_of = jnp.zeros((experts * capacity,), jnp.float32).at[slots].set(gates.reshape(-1))
    token_pad = jnp.concatenate([tokens, jnp.zeros((1, width), tokens.dtype)], axis=0)
    send = token_pad[token_of].reshape(experts, capacity, width)

    def exchange(rows):
        return lax.all_to_all(
            rows.reshape(experts, capacity, width), "expert", split_axis=0, concat_axis=0, tiled=True
        )

    block = exchange(send)
    gate_pre, up_pre, hidden, outputs = expert_forward(block, gate_mat, up_mat, down_mat)
    back_items = exchange(outputs)
    inputs = block.reshape(-1, width)
    gathered = back_items.reshape(-1, width)[slots].reshape(rows_dev, picks, width)
    mixed = jnp.sum(gates[:, :, None] * gathered.astype(jnp.float32), axis=1).astype(jnp.bfloat16)
    cot_pad = jnp.concatenate([cotangent, jnp.zeros((1, width), cotangent.dtype)], axis=0)
    cot_send = (weight_of[:, None] * cot_pad[token_of].astype(jnp.float32)).astype(jnp.bfloat16)
    slot_cot = exchange(cot_send).reshape(-1, width)
    down_part = jnp.dot(hidden.T, slot_cot, preferred_element_type=jnp.float32)
    hidden_grad = jnp.dot(slot_cot, down_mat.T, preferred_element_type=jnp.float32)
    sigma = jax.nn.sigmoid(gate_pre)
    gate_grad = (hidden_grad * up_pre * sigma * (1.0 + gate_pre * (1.0 - sigma))).astype(
        jnp.bfloat16
    )
    up_grad = (hidden_grad * gate_pre * sigma).astype(jnp.bfloat16)
    slot_grads = (
        jnp.dot(gate_grad, gate_mat.T, preferred_element_type=jnp.float32)
        + jnp.dot(up_grad, up_mat.T, preferred_element_type=jnp.float32)
    ).astype(jnp.bfloat16)
    grads_back = exchange(slot_grads)
    gate_part = jnp.dot(inputs.T, gate_grad, preferred_element_type=jnp.float32)
    up_part = jnp.dot(inputs.T, up_grad, preferred_element_type=jnp.float32)
    grad_rows = grads_back.reshape(-1, width)[slots].reshape(rows_dev, picks, width)
    input_grad = jnp.sum(grad_rows.astype(jnp.float32), axis=1).astype(jnp.bfloat16)
    return (mixed, input_grad) + relay_sums(gate_part, up_part, down_part)


def relay_sums(*parts):
    relays = lax.axis_size("pipe")
    sums = []
    for part in parts:
        part = part.astype(BF)
        if relays == 2:
            other = lax.ppermute(part, "pipe", [(0, 1), (1, 0)])
            total = (part.astype(F32) + other.astype(F32)).astype(BF)
        else:
            total = lax.psum(part, "pipe")
        sums.append(total[None])
    return tuple(sums)


def chosen_rows(ids_ref, meta, picks, capacity):
    columns = meta.T
    routes, high, low = (columns[n * picks : (n + 1) * picks] for n in range(3))
    rows = meta.shape[0]
    member, weights = [], []
    for k in range(PLANE):
        hit = routes == ids_ref[k].astype(F32)
        member.append(jnp.sum(jnp.where(hit, 1.0, 0.0), axis=0, keepdims=True))
        weights.append(
            [jnp.sum(jnp.where(hit, part, 0.0), axis=0, keepdims=True) for part in (high, low)]
        )
    stacked = jnp.concatenate(member + [jnp.zeros((16 - PLANE, rows), F32)], axis=0)
    first = lax.broadcasted_iota(jnp.int32, (rows, rows), 0)
    second = lax.broadcasted_iota(jnp.int32, (rows, rows), 1)
    ahead = jnp.where(first < second, 1.0, 0.0).astype(BF)
    rank = jnp.dot(stacked.astype(BF), ahead, preferred_element_type=F32)
    slot = lax.broadcasted_iota(jnp.int32, (capacity, rows), 0).astype(F32)
    pick, pick_high, pick_low = [], [], []
    for k in range(PLANE):
        chosen = slot == jnp.where(member[k] > 0.5, rank[k : k + 1], -1.0)
        pick.append(jnp.where(chosen, 1.0, 0.0))
        pick_high.append(jnp.where(chosen, weights[k][0], 0.0))
        pick_low.append(jnp.where(chosen, weights[k][1], 0.0))
    return [jnp.concatenate(part, axis=0) for part in (pick, pick_high, pick_low)]


def put(out_refs, n, start, picked, capacity):
    for k, out_ref in enumerate(out_refs):
        out_ref[n, start : start + capacity] = picked[k * capacity : (k + 1) * capacity]


def picked_rows(matrices, block):
    return sum(jnp.dot(m, block, preferred_element_type=F32) for m in matrices).astype(BF)


def start_kernel(ids_ref, *refs, picks, capacity):
    sources, block_ref, table_ref, turned_ref = refs[:4], *refs[4:7]
    out_refs, held, arrived = refs[7 : 7 + PLANE], refs[7 + PLANE : -1], refs[-1]
    copies = [
        pltpu.make_async_copy(source, target, arrived.at[n])
        for n, (source, target) in enumerate(zip(sources, held))
    ]
    for copy in copies:
        copy.start()
    for copy in copies:
        copy.wait()
    tokens_ref, routes_ref, gates_ref, cot_ref = held
    rows, width = tokens_ref.shape
    gates = gates_ref[...]
    high = gates.astype(BF).astype(F32)
    low = (gates - high).astype(BF).astype(F32)
    beside = [routes_ref[...].astype(F32), high, low, jnp.zeros((128 - 3 * picks, rows), F32)]
    meta = jnp.concatenate(beside, axis=0).T
    block_ref[:, :width] = tokens_ref[...]
    block_ref[:, width:] = meta.astype(BF)
    write_tables(ids_ref, meta, table_ref, turned_ref, 0, picks, capacity)
    put(out_refs, 0, 0, picked_rows([table_ref[0, 0]], tokens_ref[...]), capacity)
    rows = picked_rows([table_ref[0, 1], table_ref[0, 2]], cot_ref[...])
    put(out_refs, 0, capacity, rows, capacity)


def write_tables(ids_ref, meta, table_ref, turned_ref, n, picks, capacity):
    for m, table in enumerate(chosen_rows(ids_ref, meta, picks, capacity)):
        table_ref[n, m] = table.astype(BF)
        turned_ref[n, m] = table.T.astype(BF)


def table_shapes(count, capacity, rows):
    return [(count, 3, PLANE * capacity, rows), (count, 3, rows, PLANE * capacity)]


def start_rows(ids, tokens, routes, gates, cotangent, capacity):
    rows, width = tokens.shape
    picks = routes.shape[1]
    shapes = [(rows, width + 128)] + table_shapes(1, capacity, rows)
    shapes += [(1, 2 * capacity, width)] * PLANE
    block, table, turned, *out = pl.pallas_call(
        functools.partial(start_kernel, picks=picks, capacity=capacity),
        in_specs=[pl.BlockSpec(memory_space=pltpu.SMEM)]
        + [pl.BlockSpec(memory_space=pltpu.HBM)] * 4,
        out_shape=[jax.ShapeDtypeStruct(s, BF) for s in shapes],
        scratch_shapes=[
            pltpu.VMEM((rows, width), BF),
            pltpu.VMEM((picks, rows), routes.dtype),
            pltpu.VMEM((picks, rows), gates.dtype),
            pltpu.VMEM((rows, width), BF),
            pltpu.SemaphoreType.DMA((4,)),
        ],
        compiler_params=pltpu.CompilerParams(vmem_limit_bytes=16 << 20),
        name="start_rows",
    )(ids, *(pltpu.with_memory_space_constraint(v, pltpu.HBM) for v in (tokens, routes.T, gates.T, cotangent)))
    return block, table, turned, out


def token_kernel(ids_ref, *refs, blocks, picks, capacity):
    meta_refs, row_refs, refs = refs[:blocks], refs[blocks : 2 * blocks], refs[2 * blocks :]
    table_ref, turned_ref, *out_refs = refs
    if blocks == 2:
        *out_refs, pass_ref = out_refs
        width = row_refs[0].shape[1]
        first = ids_ref[PLANE] == 1
        pass_ref[:, :width] = jnp.where(first, row_refs[0][...], row_refs[1][...])
        pass_ref[:, width:] = jnp.where(first, meta_refs[0][...], meta_refs[1][...])
    for n in range(blocks):
        meta = meta_refs[n][...].astype(F32)
        write_tables(ids_ref, meta, table_ref, turned_ref, n, picks, capacity)
        put(out_refs, n, 0, picked_rows([table_ref[n, 0]], row_refs[n][...]), capacity)


def token_rows(ids, blocks, picks, capacity):
    rows, wide = blocks[0].shape
    width, count = wide - 128, len(blocks)
    spec = [pl.BlockSpec((rows, 128), lambda i: (0, width // 128))] * count
    spec += [pl.BlockSpec((rows, width), lambda i: (0, 0))] * count
    shapes = table_shapes(count, capacity, rows) + [(count, capacity, width)] * PLANE
    if count == 2:
        shapes.append((rows, wide))
    table, turned, *out = pl.pallas_call(
        functools.partial(token_kernel, blocks=count, picks=picks, capacity=capacity),
        grid=(1,),
        in_specs=[pl.BlockSpec(memory_space=pltpu.SMEM)] + spec,
        out_specs=[pl.BlockSpec(s, lambda i, d=len(s): (0,) * d) for s in shapes],
        out_shape=[jax.ShapeDtypeStruct(s, BF) for s in shapes],
        compiler_params=pltpu.CompilerParams(vmem_limit_bytes=16 << 20),
        name="token_rows",
    )(ids, *blocks, *blocks)
    return table, turned, out


def cot_kernel(ids_ref, table_ref, *refs, blocks):
    row_refs, out_refs = refs[:blocks], refs[blocks:]
    if blocks == 2:
        *out_refs, pass_ref = out_refs
        pass_ref[...] = jnp.where(ids_ref[PLANE] == 1, row_refs[0][...], row_refs[1][...])
    for n in range(blocks):
        rows = picked_rows([table_ref[n, 1], table_ref[n, 2]], row_refs[n][...])
        put(out_refs, n, 0, rows, out_refs[0].shape[1])


def cot_rows(ids, table, blocks):
    rows, width = blocks[0].shape
    shapes = [(len(blocks), table.shape[2] // PLANE, width)] * PLANE
    if len(blocks) == 2:
        shapes.append((rows, width))
    return pl.pallas_call(
        functools.partial(cot_kernel, blocks=len(blocks)),
        in_specs=[pl.BlockSpec(memory_space=pltpu.SMEM)]
        + [pl.BlockSpec(memory_space=pltpu.VMEM)] * (1 + len(blocks)),
        out_shape=[jax.ShapeDtypeStruct(s, BF) for s in shapes],
        compiler_params=pltpu.CompilerParams(vmem_limit_bytes=16 << 20),
        name="cot_rows",
    )(ids, table, *blocks)


def expand_kernel(flags_ref, turned_ref, *refs, blocks, extras, parts, flagged):
    row_refs, extra_refs, out_refs = refs[:PLANE], refs[PLANE : PLANE + extras], refs[-blocks:]
    for n in range(blocks):
        rows = jnp.concatenate([ref[n] for ref in row_refs], axis=0)
        total = sum(jnp.dot(turned_ref[n, m], rows, preferred_element_type=F32) for m in parts)
        for ref in extra_refs:
            extra = ref[...].astype(F32)
            total += jnp.where(flags_ref[n] == 1, extra, 0.0) if flagged else extra
        out_refs[n][...] = total.astype(BF)


def expand(turned, rows, weighted, extras=(), flags=None):
    blocks, _, width = rows[0].shape
    rows_dev, slots = turned.shape[2:]
    work = 2 * blocks * rows_dev * slots * width * (2 if weighted else 1)
    moved = 2 * width * (blocks * (slots + rows_dev) + len(extras) * rows_dev)
    return pl.pallas_call(
        functools.partial(
            expand_kernel,
            blocks=blocks,
            extras=len(extras),
            parts=(1, 2) if weighted else (0,),
            flagged=flags is not None,
        ),
        in_specs=[pl.BlockSpec(memory_space=pltpu.SMEM)]
        + [pl.BlockSpec(memory_space=pltpu.VMEM)] * (1 + len(rows) + len(extras)),
        out_shape=[jax.ShapeDtypeStruct((rows_dev, width), BF)] * blocks,
        compiler_params=pltpu.CompilerParams(vmem_limit_bytes=16 << 20),
        cost_estimate=pl.CostEstimate(flops=work, bytes_accessed=moved, transcendentals=0),
        name="expand",
    )(jnp.zeros((2,), jnp.int32) if flags is None else flags, turned, *rows, *extras)


def nt_dot(a, b):
    return lax.dot_general(a, b, (((1,), (1,)), ((), ())), preferred_element_type=F32)


def forward_kernel(*refs, first):
    row_refs, (gate_ref, up_ref, down_ref), refs = refs[:PLANE], refs[PLANE : PLANE + 3], refs[PLANE + 3 :]
    gate_out, up_out, hidden_out, rows_out, *out_refs = refs
    count, capacity, width = out_refs[0].shape
    inputs = jnp.concatenate(
        [ref[n, :capacity] for ref in row_refs for n in range(count)], axis=0
    )
    rows_out[...] = inputs
    gate_pre = jnp.dot(inputs, gate_ref[...], preferred_element_type=F32)
    up_pre = jnp.dot(inputs, up_ref[...], preferred_element_type=F32)
    gate_out[...] = gate_pre
    up_out[...] = up_pre
    hidden = (gate_pre * jax.nn.sigmoid(gate_pre) * up_pre).astype(BF)
    hidden_out[...] = hidden.astype(F32).T.astype(BF)
    outputs = jnp.dot(hidden, down_ref[...], preferred_element_type=F32).astype(BF)
    for k, out_ref in enumerate(out_refs):
        for n in range(count):
            at = (k * count + n) * capacity
            out_ref[n] = outputs[at : at + capacity]


def forward(rows, capacity, gate_mat, up_mat, down_mat):
    count, _, width = rows[0].shape
    inner = gate_mat.shape[1]
    total = PLANE * count * capacity
    return pl.pallas_call(
        functools.partial(forward_kernel, first=capacity),
        out_shape=[
            jax.ShapeDtypeStruct((total, inner), F32),
            jax.ShapeDtypeStruct((total, inner), F32),
            jax.ShapeDtypeStruct((inner, total), BF),
            jax.ShapeDtypeStruct((total, width), BF),
        ]
        + [jax.ShapeDtypeStruct((count, capacity, width), BF)] * PLANE,
        compiler_params=pltpu.CompilerParams(vmem_limit_bytes=24 << 20),
        cost_estimate=pl.CostEstimate(
            flops=6 * total * width * inner,
            bytes_accessed=6 * width * inner + 6 * total * width + 10 * total * inner,
            transcendentals=total * inner,
        ),
        name="expert_forward",
    )(*rows, gate_mat, up_mat, down_mat)


def backward_kernel(*refs, skip):
    cot_refs, refs = refs[:PLANE], refs[PLANE:]
    gate_pre_ref, up_pre_ref, gate_ref, up_ref, down_ref, *refs = refs
    gate_out, up_out, rows_out, *out_refs = refs
    count, capacity, width = out_refs[0].shape
    cots = jnp.concatenate(
        [ref[n, skip : skip + capacity] for ref in cot_refs for n in range(count)], axis=0
    )
    rows_out[...] = cots
    hidden_grad = nt_dot(cots, down_ref[...])
    gate_pre, up_pre = gate_pre_ref[...], up_pre_ref[...]
    sigma = jax.nn.sigmoid(gate_pre)
    gate_grad = (hidden_grad * up_pre * sigma * (1.0 + gate_pre * (1.0 - sigma))).astype(BF)
    up_grad = (hidden_grad * gate_pre * sigma).astype(BF)
    gate_out[...] = gate_grad.astype(F32).T.astype(BF)
    up_out[...] = up_grad.astype(F32).T.astype(BF)
    grads = (nt_dot(gate_grad, gate_ref[...]) + nt_dot(up_grad, up_ref[...])).astype(BF)
    for k, out_ref in enumerate(out_refs):
        for n in range(count):
            at = (k * count + n) * capacity
            out_ref[n] = grads[at : at + capacity]


def backward(cots, skip, capacity, gate_pre, up_pre, gate_mat, up_mat, down_mat):
    count, _, width = cots[0].shape
    total, inner = gate_pre.shape
    return pl.pallas_call(
        functools.partial(backward_kernel, skip=skip),
        out_shape=[
            jax.ShapeDtypeStruct((inner, total), BF),
            jax.ShapeDtypeStruct((inner, total), BF),
            jax.ShapeDtypeStruct((total, width), BF),
        ]
        + [jax.ShapeDtypeStruct((count, capacity, width), BF)] * PLANE,
        compiler_params=pltpu.CompilerParams(vmem_limit_bytes=24 << 20),
        cost_estimate=pl.CostEstimate(
            flops=6 * total * width * inner,
            bytes_accessed=6 * width * inner + 6 * total * width + 12 * total * inner,
            transcendentals=total * inner,
        ),
        name="expert_backward",
    )(*cots, gate_pre, up_pre, gate_mat, up_mat, down_mat)


def partial_kernel(*refs):
    out_ref = refs[-1]
    chunks = (len(refs) - 1) // 5
    hidden, gate_grad, up_grad, inputs, cots = (
        refs[n * chunks : (n + 1) * chunks] for n in range(5)
    )
    for n, (left, right) in enumerate(((gate_grad, inputs), (up_grad, inputs), (hidden, cots))):
        total = sum(
            jnp.dot(a[...], b[...], preferred_element_type=F32) for a, b in zip(left, right)
        )
        out_ref[n] = total.astype(BF)


def partial_sums(hidden, gate_grad, up_grad, inputs, cots):
    inner, width = hidden[0].shape[0], inputs[0].shape[1]
    total = sum(a.shape[0] for a in inputs)
    tile = min(512, width)
    small = [*hidden, *gate_grad, *up_grad]
    large = [*inputs, *cots]
    return pl.pallas_call(
        partial_kernel,
        grid=(width // tile,),
        in_specs=[pl.BlockSpec(a.shape, lambda i: (0, 0)) for a in small]
        + [pl.BlockSpec((a.shape[0], tile), lambda i: (0, i)) for a in large],
        out_specs=pl.BlockSpec((3, inner, tile), lambda i: (0, 0, i)),
        out_shape=pltpu.HBM((3, inner, width), BF),
        compiler_params=pltpu.CompilerParams(vmem_limit_bytes=24 << 20),
        cost_estimate=pl.CostEstimate(
            flops=6 * total * inner * width,
            bytes_accessed=6 * total * inner + 4 * total * width + 6 * inner * width,
            transcendentals=0,
        ),
        name="partial_sums",
    )(*small, *large)


def turn_kernel(*refs):
    *sum_refs, gate_ref, up_ref, down_ref = refs
    for n, out_ref in enumerate((gate_ref, up_ref, down_ref)):
        total = sum(ref[n].astype(F32) for ref in sum_refs)
        out_ref[0] = (total if n == 2 else total.T).astype(BF)


def weight_outputs(*sums):
    _, inner, width = sums[0].shape
    tile = min(512, width)
    return pl.pallas_call(
        turn_kernel,
        grid=(width // tile,),
        in_specs=[pl.BlockSpec((3, inner, tile), lambda i: (0, 0, i))] * len(sums),
        out_specs=[
            pl.BlockSpec((1, tile, inner), lambda i: (0, i, 0)),
            pl.BlockSpec((1, tile, inner), lambda i: (0, i, 0)),
            pl.BlockSpec((1, inner, tile), lambda i: (0, 0, i)),
        ],
        out_shape=[
            jax.ShapeDtypeStruct((1, width, inner), BF),
            jax.ShapeDtypeStruct((1, width, inner), BF),
            jax.ShapeDtypeStruct((1, inner, width), BF),
        ],
        compiler_params=pltpu.CompilerParams(vmem_limit_bytes=16 << 20),
        cost_estimate=pl.CostEstimate(
            flops=6 * inner * width,
            bytes_accessed=6 * inner * width * (1 + len(sums)),
            transcendentals=0,
        ),
        name="weight_outputs",
    )(*(pltpu.with_memory_space_constraint(v, pltpu.HBM) for v in sums))


def plane_plan(tokens, routes, gates, cotangent, w_gate, w_up, w_down):
    rows_dev, width = tokens.shape
    picks = routes.shape[1]
    experts = lax.axis_size("expert")
    capacity = rows_dev * picks // experts
    mats = (w_gate[0], w_up[0], w_down[0])
    here = lax.axis_index("expert")
    level, place = here // PLANE, here % PLANE
    odd = level % 2
    ids = jnp.stack([level * PLANE + (place ^ k) for k in range(PLANE)] + [odd])

    def permute(value, step):
        pairs = [(i, step(i // PLANE) % LEVELS * PLANE + i % PLANE) for i in range(experts)]
        return lax.ppermute(value, "expert", pairs)

    def from_above(value):
        return permute(value, lambda n: n - 1)

    def from_below(value):
        return permute(value, lambda n: n + 1)

    def swap(value):
        return permute(value, lambda n: n ^ 1)

    stages = []

    def across(rows, *deps):
        sent = tuple(rows[1:])
        if stages or deps:
            sent, *_ = lax.optimization_barrier((sent, *stages[-1:], *deps))
        moved = {
            k: lax.ppermute(sent[k - 1], "expert", [(i, i ^ k) for i in range(experts)])
            for k in (3, 1, 2)
        }
        stages.append(tuple(moved[k] for k in range(1, PLANE)))
        return [rows[0], *stages[-1]]

    block, table_a, turned_a, rows_a = start_rows(ids, tokens, routes, gates, cotangent, capacity)
    rows_a = across(rows_a)
    above, below = from_above(block), from_below(block)
    table_b, turned_b, (*rows_b, far) = token_rows(ids, [above, below], picks, capacity)
    far = swap(far)
    rows_b = across(rows_b)
    later, far = lax.optimization_barrier((cotangent, far))
    cot_above, cot_below = from_above(later), from_below(later)
    table_c, turned_c, rows_c = token_rows(ids, [far], picks, capacity)
    rows_c = across(rows_c)
    *cots_b, cot_far = cot_rows(ids, table_b, [cot_above, cot_below])
    cot_far = swap(cot_far)
    cots_b = across(cots_b)

    saved = [forward(rows, capacity, *mats) for rows in (rows_a, rows_b, rows_c)]
    outs = [s[4:] for s in saved]

    def back(cots, skip, forth):
        return backward(cots, skip, capacity, forth[0], forth[1], *mats)

    back_a = back(rows_a, capacity, saved[0])
    cots_c = across(cot_rows(ids, table_c, [cot_far]), saved, back_a)
    back_b = back(cots_b, 0, saved[1])
    mixed_c = across(outs[2], back_b)
    back_c = back(cots_c, 0, saved[2])
    backs = (back_a, back_b, back_c)
    partial = partial_sums(
        [s[2] for s in saved],
        [b[0] for b in backs],
        [b[1] for b in backs],
        [s[3] for s in saved],
        [b[2] for b in backs],
    )
    grads_c = across(back_c[3:], partial)
    passed = jnp.stack([odd, 1 - odd])

    def send_near(rows, weighted, far, *deps):
        near = expand(turned_b, rows, weighted, [far], passed)
        near, *_ = lax.optimization_barrier((near, *deps))
        return from_below(near[0]), from_above(near[1])

    mixed_far = swap(*expand(turned_c, mixed_c, True))
    sent, _ = lax.optimization_barrier((partial, mixed_c))
    other = lax.ppermute(sent, "pipe", [(0, 1), (1, 0)])
    mixed_b = across(outs[1])
    grads_far = swap(*expand(turned_c, grads_c, False))
    weight_grads = weight_outputs(partial, other)
    grads_b = across(back_b[3:], mixed_far, grads_far, weight_grads)
    mixed_near = send_near(mixed_b, True, mixed_far, grads_far)
    mixed_a = across(outs[0])
    grads_near = send_near(grads_b, False, grads_far, mixed_near)
    grads_a = across(back_a[3:], mixed_near)
    mixed = expand(turned_a, mixed_a, True, mixed_near)
    input_grad = expand(turned_a, grads_a, False, grads_near)
    return (*mixed, *input_grad, *weight_grads)


def on_device(tokens, routes, *rest):
    experts, picks = lax.axis_size("expert"), routes.shape[1]
    if experts == LEVELS * PLANE and lax.axis_size("pipe") == 2 and experts <= 2 * picks:
        return plane_plan(tokens, routes, *rest)
    return direct_plan(tokens, routes, *rest)


def solution(mesh):
    rows, stack = P(("pipe", "expert"), None), P("expert", None, None)
    return jax.shard_map(
        on_device,
        mesh=mesh,
        in_specs=(rows, rows, rows, rows, stack, stack, stack),
        out_specs=(rows, rows, stack, stack, stack),
        check_vma=False,
    )
```
